32 devices in a mesh: gx: 8 (over z, x), gy: 4 (over y, core).
Axes of the slice: x: 2, y: 2, z: 4, core: 2. Of those that a mesh axis runs over, the one named last changes fastest.
Arguments:
- populations: float32 [19, 256, 2048], P(None, 'gx', 'gy'), may hold values from 0 to 0.7, as said below
- positions: float32 [768, 3, 642], P(('gx', 'gy')), may hold values from -3 to 31, as said below
- stiffness: float32 [768], P(('gx', 'gy')), may hold values from 0.002 to 0.02
- membrane_shape: float32 [3, 642], replicated, may hold values from -6 to 6
- neighbours: int32 [642, 6], replicated, may hold values from 0 to 641, as said below
- home_tile: int32 [768], P(('gx', 'gy')), may hold values from 0 to 31, as said below
Outputs:
- populations_out: float32 [19, 256, 2048], P(None, 'gx', 'gy')
- displacement: float32 [768, 3, 642], P(('gx', 'gy'))
- force_density: float32 [3, 256, 2048], P(None, 'gx', 'gy')
The draws below stay inside these ranges and needn't reach their ends.
Inputs may be any that keep to these rules, and one draw needn't show every extreme that they name: `populations`: every entry is positive. `positions`: the first coordinate lies within [1, 31], the second within [1, 31]; the third is taken modulo 16. `neighbours`: row v never names v. `home_tile`: cells are owned in blocks of 24 in gx+gy order; the home tile of a cell owned at gx index a has gx index a - 1, a or a + 1 (cyclically) and any gy index, numbered gx index times the number of gy devices plus gy index; at most 4 cells of one device share a home tile, and in every device some home tile has exactly 4 of them.
All inputs are finite; a program needn't handle non-finite values.
Results may differ from the reference program's by a relative error of at most 0.0022.
Values sent between devices are 32-bit elements; how exact they have to be, the bound alone decides.
No kernel may reach another device: no remote copies, remote signals or barrier semaphores. Data moves between devices by JAX's collectives and lax.ppermute only.
A program may use at most 64 MiB of HBM per device.

```python
import math
import jax
import jax.numpy as jnp
from jax import lax

CX = 32
CY = 32
CZ = 16
V = 642
NB = 6
CELL_DEV = 24
CAP = 4
STEPS = 2
NX = 256
NY = 128
NCELL = 768
N_GX = 8
N_GY = 4


LATTICE_WEIGHT = [1.0 / 3.0] + [1.0 / 18.0] * 6 + [1.0 / 36.0] * 12


def draw_populations(key, part):
    weights = jnp.asarray(LATTICE_WEIGHT, jnp.float32)[:, None, None]
    full_shape = (19, NX, NY * CZ)
    roughness = jax.random.uniform(key, full_shape, jnp.float32, 0.2, 1.8)
    return weights * roughness


def draw_positions(key, part):
    subkeys = jax.random.split(key, 2)
    lowest = jnp.asarray([4.0, 4.0, 0.0], jnp.float32)[:, None]
    highest = jnp.asarray([CX - 4.0, CY - 4.0, CZ * 1.0], jnp.float32)[:, None]
    centers = lowest + (highest - lowest) * jax.random.uniform(subkeys[0], (NCELL, 3, 1), jnp.float32)
    scatter_noise = jax.random.uniform(subkeys[1], (NCELL, 3, V), jnp.float32, -1.0, 1.0)
    return centers + 3.0 * scatter_noise


def draw_neighbours(key, part):
    hopping = jax.random.randint(key, (V, NB), 1, V, jnp.int32)
    return (jnp.arange(V, dtype=jnp.int32)[:, None] + hopping) % V


def draw_home_tile(key, part):
    slots_total = 3 * N_GY * CAP

    def one_owner(owner):
        subkeys = jax.random.split(jax.random.fold_in(key, owner), 3)
        full_group = jax.random.randint(subkeys[0], (), 0, 3 * N_GY, jnp.int32)
        scores = jax.random.permutation(subkeys[1], slots_total).astype(jnp.int32)
        groups = jnp.arange(slots_total, dtype=jnp.int32) // CAP
        scores = jnp.where(groups == full_group, scores - slots_total, scores)
        chosen = jnp.argsort(scores)[:CELL_DEV].astype(jnp.int32)
        chosen = jax.random.permutation(subkeys[2], chosen)
        group = chosen // CAP
        offset = group // N_GY
        target_y = group % N_GY
        owner_x = owner // N_GY
        return (owner_x + offset - 1) % N_GX * N_GY + target_y
    return jax.vmap(one_owner)(jnp.arange(N_GX * N_GY, dtype=jnp.int32)).reshape(-1)


def steps_of(rng, dims, pieces, low, high):
    level = 1.0
    for position, shards_of in pieces:
        draws = jax.random.uniform(jax.random.fold_in(jax.random.fold_in(rng, 6), position), (shards_of,), jnp.float32, low / len(pieces), high / len(pieces))
        level = level * jnp.repeat(jnp.exp(draws), dims[position] // shards_of).reshape((-1,) + (1,) * (len(dims) - 1 - position))
    return level


def bell_draw(key, dims, spread, limit, kind=jnp.bfloat16):
    values = jax.random.normal(key, dims, jnp.float32) * spread
    return jnp.minimum(jnp.maximum(values, -limit), limit).astype(kind)


def setup_inputs(seed: int = 0) -> dict:
    key_list = jax.random.split(jax.random.key(seed), 7)
    return {
        "populations": draw_populations(jax.random.fold_in(key_list[6], 71), 0),
        "positions": draw_positions(jax.random.fold_in(key_list[6], 71), 0),
        "stiffness": jnp.clip(jnp.exp(math.log(0.02) - 2.30258502 * jax.random.uniform(key_list[2], (NCELL,), jnp.float32) ** steps_of(key_list[2], (NCELL,), ((0, 32),), -0.2, 0.2)), 0.002, 0.02),
        "membrane_shape": bell_draw(key_list[3], (3, V), 1.5, 6.0, jnp.float32),
        "neighbours": draw_neighbours(jax.random.fold_in(key_list[6], 71), 0),
        "home_tile": draw_home_tile(jax.random.fold_in(key_list[6], 71), 0),
    }


LATTICE_VELOCITY = [[0, 0, 0], [1, 0, 0], [-1, 0, 0], [0, 1, 0], [0, -1, 0], [0, 0, 1], [0, 0, -1], [1, 1, 0], [-1, -1, 0], [1, -1, 0], [-1, 1, 0], [1, 0, 1], [-1, 0, -1], [1, 0, -1], [-1, 0, 1], [0, 1, 1], [0, -1, -1], [0, 1, -1], [0, -1, 1]]
LATTICE_WEIGHT = [1.0 / 3.0] + [1.0 / 18.0] * 6 + [1.0 / 36.0] * 12
RELAX_RATE = 1.25
PUSH_SCALE = 0.05
TETHER_GAIN = 2.0


def stiffness_matrix(neighbours):
    vertices = neighbours.shape[0]
    columns = jnp.arange(vertices, dtype=jnp.int32)
    linked = jnp.sum((neighbours[:, :, None] == columns[None, None, :]).astype(jnp.float32), axis=1)
    linked = linked + linked.T
    degree = jnp.sum(linked, axis=1)
    return jnp.diag(degree + TETHER_GAIN) - linked


def membrane_force(places, stiffness, membrane_shape, matrix):
    center = jnp.mean(places, axis=2, keepdims=True)
    strain = places - center - membrane_shape[None]
    vertices = places.shape[2]
    pulled = jnp.dot(strain.reshape(-1, vertices), matrix, precision=lax.Precision.HIGHEST, preferred_element_type=jnp.float32)
    return -stiffness[:, None, None] * pulled.reshape(places.shape)


def moments(populations):
    velocity_table = jnp.asarray(LATTICE_VELOCITY, jnp.float32)
    density = jnp.sum(populations, axis=0)
    momentum = jnp.tensordot(velocity_table.T, populations, axes=1, precision=lax.Precision.HIGHEST)
    return density, momentum


def fluid_velocity(populations, push):
    density, momentum = moments(populations)
    return (momentum + 0.5 * push) / density


def collide(populations, push):
    velocity_table = jnp.asarray(LATTICE_VELOCITY, jnp.float32)
    weights = jnp.asarray(LATTICE_WEIGHT, jnp.float32)[:, None, None]
    density, momentum = moments(populations)
    velocity = (momentum + 0.5 * push) / density
    along = jnp.tensordot(velocity_table, velocity, axes=1, precision=lax.Precision.HIGHEST)
    push_along = jnp.tensordot(velocity_table, push, axes=1, precision=lax.Precision.HIGHEST)
    speed_square = jnp.sum(velocity * velocity, axis=0)
    push_dot = jnp.sum(velocity * push, axis=0)
    balance = weights * density * (1.0 + 3.0 * along + 4.5 * along * along - 1.5 * speed_square)
    source = (1.0 - 0.5 * RELAX_RATE) * weights * (3.0 * (push_along - push_dot) + 9.0 * along * push_along)
    return populations - RELAX_RATE * (populations - balance) + source


def stream_all(post):
    shaped = post.reshape(19, NX, NY, CZ)
    moved = [jnp.roll(shaped[member], tuple(LATTICE_VELOCITY[member]), axis=(0, 1, 2)) for member in range(19)]
    return jnp.stack(moved).reshape(post.shape)


def axis_hats(coordinate, extent):
    floored = jnp.floor(coordinate)
    fraction = coordinate - floored
    base_index = floored.astype(jnp.int32)
    hat_pairs = []
    for advance, weight in ((0, 1.0 - fraction), (1, fraction)):
        corner = base_index + advance
        inside = (corner >= 0) & (corner < extent)
        hat_pairs.append((jnp.clip(corner, 0, extent - 1), jnp.where(inside, weight, 0.0)))
    return hat_pairs


def periodic_hats(coordinate, extent):
    wrapped = jnp.mod(coordinate, extent * 1.0)
    floored = jnp.floor(wrapped)
    fraction = wrapped - floored
    base_index = floored.astype(jnp.int32)
    return [(base_index % extent, 1.0 - fraction), ((base_index + 1) % extent, fraction)]


def rounded(values):
    return lax.optimization_barrier(values.astype(jnp.bfloat16)).astype(jnp.float32)


def tile_corners(places, home_tile):
    tile_x = home_tile // N_GY
    tile_y = home_tile % N_GY
    anchor_x = (tile_x * CX)[:, None]
    anchor_y = (tile_y * CY)[:, None]
    x_hats = axis_hats(places[:, 0], CX)
    y_hats = axis_hats(places[:, 1], CY)
    z_hats = periodic_hats(places[:, 2], CZ)
    plane_pairs = []
    for y_index, y_weight in y_hats:
        for z_index, z_weight in z_hats:
            table = rounded(y_weight * z_weight)
            columns = ((anchor_y + y_index) * CZ + z_index).reshape(-1)
            plane_pairs.append((columns, table))
    row_pairs = [((anchor_x + x_index).reshape(-1), x_weight) for x_index, x_weight in x_hats]
    return row_pairs, plane_pairs


def spread_all(places, force, home_tile):
    row_pairs, plane_pairs = tile_corners(places, home_tile)
    grid = jnp.zeros((3, NX, NY * CZ), jnp.float32)
    for rows, x_weight in row_pairs:
        lifted = rounded(force * x_weight[:, None, :])
        for columns, table in plane_pairs:
            values = (lifted * table[:, None, :]).transpose(1, 0, 2).reshape(3, -1)
            grid = grid.at[:, rows, columns].add(values)
    return grid


def sample_all(places, velocity, home_tile):
    row_pairs, plane_pairs = tile_corners(places, home_tile)
    count_cells = places.shape[0]
    vertices = places.shape[2]
    result = jnp.zeros(places.shape, jnp.float32)
    for rows, x_weight in row_pairs:
        inner = jnp.zeros((3, count_cells * vertices), jnp.float32)
        for columns, table in plane_pairs:
            inner = inner + velocity[:, rows, columns].astype(jnp.float32) * table.reshape(-1)[None]
        result = result + x_weight[:, None, :] * inner.reshape(3, count_cells, vertices).transpose(1, 0, 2)
    return result


def reference(populations, positions, stiffness, membrane_shape, neighbours, home_tile):
    matrix = stiffness_matrix(neighbours)
    starting = positions
    density_grid = jnp.zeros((3, NX, NY * CZ), jnp.float32)
    for _ in range(STEPS):
        force = membrane_force(positions, stiffness, membrane_shape, matrix)
        density_grid = spread_all(positions, force, home_tile)
        push = PUSH_SCALE * density_grid
        populations = stream_all(collide(populations, push))
        velocity = fluid_velocity(populations, push).astype(jnp.bfloat16)
        positions = positions + sample_all(positions, velocity, home_tile)
    return populations, positions - starting, density_grid
```

```python
import functools

import jax
import jax.numpy as jnp
from jax import lax
from jax.experimental import pallas as pl
from jax.experimental.pallas import tpu as pltpu
from jax.sharding import PartitionSpec as P

CZ = 16
CAP = 4
STEPS = 2

LATTICE_VELOCITY = [
    [0, 0, 0],
    [1, 0, 0],
    [-1, 0, 0],
    [0, 1, 0],
    [0, -1, 0],
    [0, 0, 1],
    [0, 0, -1],
    [1, 1, 0],
    [-1, -1, 0],
    [1, -1, 0],
    [-1, 1, 0],
    [1, 0, 1],
    [-1, 0, -1],
    [1, 0, -1],
    [-1, 0, 1],
    [0, 1, 1],
    [0, -1, -1],
    [0, 1, -1],
    [0, -1, 1],
]
LATTICE_WEIGHT = [1.0 / 3.0] + [1.0 / 18.0] * 6 + [1.0 / 36.0] * 12
RIGHT_MOVERS = [1, 7, 9, 11, 13]
LEFT_MOVERS = [2, 8, 10, 12, 14]
UPWARD_MOVERS = [3, 7, 10, 15, 17]
DOWNWARD_MOVERS = [4, 8, 9, 16, 18]
RELAX_RATE = 1.25
PUSH_SCALE = 0.05
TETHER_GAIN = 2.0
LANES = 128
F32 = jnp.float32
BF16 = jnp.bfloat16
SMEM = pltpu.SMEM
VMEM = pltpu.VMEM


def spec(space):
    return pl.BlockSpec(memory_space=space)


def call(kernel, outs, ins, scratch=(), cost=None, limit=None):
    return pl.pallas_call(
        kernel,
        out_shape=[jax.ShapeDtypeStruct(s, d) for s, d, _ in outs],
        in_specs=[spec(m) for m in ins],
        out_specs=[spec(m) for _, _, m in outs],
        scratch_shapes=list(scratch),
        compiler_params=pltpu.CompilerParams(vmem_limit_bytes=limit or (24 << 20)),
        cost_estimate=cost,
    )


def lane_index(shape):
    return lax.broadcasted_iota(jnp.int32, shape, len(shape) - 1)


def row_index(shape):
    return lax.broadcasted_iota(jnp.int32, shape, len(shape) - 2)


class Sizes:
    def __init__(self, cells, vertices, width_x, plane, devices_x, devices_y):
        self.cells = cells
        self.vertices = vertices
        self.width_x = width_x
        self.plane = plane
        self.devices_x = devices_x
        self.devices_y = devices_y
        self.main = vertices - vertices % LANES
        self.tail = vertices - self.main
        self.full = self.main + LANES
        self.message = 3 * self.main + LANES
        self.center = devices_y * CAP
        self.slots = 3 * devices_y * CAP
        self.width_y = plane // CZ


def cell_places(z, home_ref, count_ref):
    own_x = lax.axis_index("gx")
    own_y = lax.axis_index("gy")
    for g in range(3 * z.devices_y):
        count_ref[g] = 0
    found = []
    for n in range(z.cells):
        home = home_ref[n]
        target_x = lax.div(home, z.devices_y)
        target_y = lax.rem(home, z.devices_y)
        side = lax.rem(target_x - own_x + 1 + z.devices_x, z.devices_x)
        turn = lax.rem(target_y - own_y + z.devices_y, z.devices_y)
        group = side * z.devices_y + turn
        rank = count_ref[group]
        count_ref[group] = rank + 1
        found.append((group, rank))
    return found


def pack_kernel(z, home_ref, stiff_ref, places_ref, *rest):
    left_ref, right_ref = rest[:2]
    center_refs = rest[2 : 2 + z.devices_y]
    table_ref, count_ref = rest[2 + z.devices_y :]
    table_ref[...] = jnp.zeros_like(table_ref)
    lane = lane_index((1, LANES))
    zeros = jnp.zeros((1, LANES - z.tail), F32)
    for n, (group, rank) in enumerate(cell_places(z, home_ref, count_ref)):
        ends = jnp.where(lane == 3 * z.tail, stiff_ref[n], 0.0)
        parts = []
        for c in range(3):
            line = places_ref[n, c : c + 1, :]
            parts.append(line[:, : z.main])
            end = jnp.concatenate([line[:, z.main :], zeros], axis=1)
            ends = ends + (end if c == 0 else pltpu.roll(end, c * z.tail, 1))
        table_ref[group, pl.ds(rank, 1), :] = jnp.concatenate(parts + [ends], axis=1)
    d = z.devices_y
    left_ref[...] = table_ref[0:d]
    right_ref[...] = table_ref[2 * d : 3 * d]
    for r in range(d):
        center_refs[r][...] = table_ref[d + r]


def unpack_kernel(z, home_ref, places_ref, left_ref, right_ref, *rest):
    center_refs = rest[: z.devices_y]
    out_ref, table_ref, count_ref = rest[z.devices_y :]
    d = z.devices_y
    table_ref[0:d] = left_ref[...]
    table_ref[2 * d : 3 * d] = right_ref[...]
    for r in range(d):
        table_ref[d + r] = center_refs[r][...]
    for n, (group, rank) in enumerate(cell_places(z, home_ref, count_ref)):
        line = table_ref[group, pl.ds(rank, 1), :]
        ends = line[:, 3 * z.main :]
        for c in range(3):
            end = ends if c == 0 else pltpu.roll(ends, LANES - c * z.tail, 1)
            whole = jnp.concatenate([line[:, c * z.main : (c + 1) * z.main], end], axis=1)
            out_ref[n, c : c + 1, :] = whole[:, : z.vertices] - places_ref[n, c : c + 1, :]


def matrix_kernel(z, near_ref, near_t_ref, link_ref, degree_ref):
    near = near_ref[...]
    near_t = near_t_ref[...]
    count = near.shape[1]
    lane = lane_index((z.full, LANES))
    row = row_index((z.full, LANES))
    for t in range(z.full // LANES):
        total = jnp.zeros((z.full, LANES), F32)
        for b in range(count):
            total += jnp.where(near[:, b : b + 1] == lane + t * LANES, 1.0, 0.0)
            total += jnp.where(near_t[b : b + 1, t * LANES : (t + 1) * LANES] == row, 1.0, 0.0)
        link_ref[:, t * LANES : (t + 1) * LANES] = total.astype(BF16)
        degree_ref[:, t * LANES : (t + 1) * LANES] = (
            jnp.sum(total, axis=0, keepdims=True) + TETHER_GAIN
        )


def list_active(flags, first, last, ids_ref, start, count_at):
    def step(s, state):
        count, empty = state
        filled = flags(s) > 0.0

        @pl.when(filled)
        def _():
            ids_ref[start + count] = s

        return (
            jnp.where(filled, count + 1, count),
            jnp.where(filled, empty, s),
        )

    count, empty = lax.fori_loop(first, last, step, (jnp.int32(0), jnp.int32(first)))

    @pl.when(lax.rem(count, 2) == 1)
    def _():
        ids_ref[start + count] = empty

    ids_ref[count_at] = lax.div(count + 1, 2)


def split_message(z, line_ref, at, places_ref, ends_ref, slot):
    value = line_ref[...] if at is None else line_ref[at]
    for c in range(3):
        places_ref[c, slot : slot + CAP, : z.main] = value[:, c * z.main : (c + 1) * z.main]
    ends_ref[slot : slot + CAP, :] = value[:, 3 * z.main :]


def place_tails(z, ends_ref, places_ref, stiff_ref):
    ends = ends_ref[...]
    lane = lane_index(ends.shape)
    for c in range(3):
        end = ends if c == 0 else pltpu.roll(ends, LANES - c * z.tail, 1)
        places_ref[c, :, z.main :] = jnp.where(lane < z.tail, end, 0.0)
    stiff_ref[...] = jnp.broadcast_to(ends[:, 3 * z.tail : 3 * z.tail + 1], ends.shape)


def forces(z, places_ref, stiff_ref, shape_ref, link_ref, degree_ref, force_ref):
    rows = places_ref.shape[1]
    lane = lane_index((rows, z.full))
    inside = lane < z.vertices
    parts = []
    for c in range(3):
        x = places_ref[c]
        mean = jnp.sum(x, axis=1, keepdims=True) * (1.0 / z.vertices)
        parts.append(jnp.where(inside, x - mean - shape_ref[c : c + 1, :], 0.0))
    strain = jnp.concatenate(parts, axis=0)
    high = strain.astype(BF16)
    rest = strain - high.astype(F32)
    low = rest.astype(BF16)
    link = link_ref[...]
    linked = jnp.dot(high, link, preferred_element_type=F32) + jnp.dot(
        low, link, preferred_element_type=F32
    )
    pulled = degree_ref[...] * (high.astype(F32) + low.astype(F32)) - linked
    stiff = stiff_ref[:, 0:1]
    for c in range(3):
        force_ref[c] = -stiff * pulled[c * rows : (c + 1) * rows]


def tails_to_lanes(z, ref, c):
    ends = ref[c, :, z.main :]
    lane = lane_index(ends.shape)
    row = row_index(ends.shape)
    picked = jnp.zeros_like(ends)
    for t in range(z.tail):
        picked = jnp.where(lane == row * z.tail + t, ends[:, t : t + 1], picked)
    return jnp.sum(picked, axis=0, keepdims=True)


def hat_tables(z, x, y, depth, plane_ref, at):
    width = x.shape[1]
    steps_x = row_index((z.width_x, width)).astype(F32)
    steps_y = steps_x if z.width_y == z.width_x else row_index((z.width_y, width)).astype(F32)
    steps_z = row_index((CZ, width)).astype(F32)
    hat_x = jnp.maximum(0.0, 1.0 - jnp.abs(x - steps_x))
    hat_y = jnp.maximum(0.0, 1.0 - jnp.abs(y - steps_y))
    wrapped = depth - CZ * jnp.floor(depth * (1.0 / CZ))
    gap = jnp.abs(wrapped - steps_z)
    hat_z = jnp.maximum(0.0, 1.0 - jnp.minimum(gap, CZ - gap))
    for j in range(z.width_y):
        plane_ref[j * CZ : (j + 1) * CZ, at : at + width] = (hat_y[j : j + 1] * hat_z).astype(BF16)
    return hat_x


def spread(z, places_ref, force_ref, ids_ref, start, pairs, grid_ref, plane_ref, lift_ref, tails):
    def contract(width):
        return lax.dot_general(
            lift_ref[:, :width],
            plane_ref[:, :width],
            (((1,), (1,)), ((), ())),
            preferred_element_type=F32,
        )

    def fill(line, pull, at):
        hat_x = hat_tables(z, *line, plane_ref, at)
        width = line[0].shape[1]
        for c in range(3):
            lift_ref[c * z.width_x : (c + 1) * z.width_x, at : at + width] = (
                pull[c] * hat_x
            ).astype(BF16)

    def step(p, carry):
        for h in range(2):
            s = ids_ref[start + 2 * p + h]
            line = [places_ref[c, pl.ds(s, 1), : z.main] for c in range(3)]
            pull = [force_ref[c, pl.ds(s, 1), : z.main] for c in range(3)]
            fill(line, pull, h * z.main)
        grid_ref[...] += contract(2 * z.main)
        return carry

    lax.fori_loop(0, pairs, step, 0)
    if tails:
        line = [tails_to_lanes(z, places_ref, c) for c in range(3)]
        pull = [tails_to_lanes(z, force_ref, c) for c in range(3)]
        fill(line, pull, 0)
        grid_ref[...] += contract(LANES)


def sample(z, places_ref, flow_ref, ids_ref, start, pairs, plane_ref):
    def step(p, carry):
        hats = []
        slots = [ids_ref[start + 2 * p + h] for h in range(2)]
        lines = [[places_ref[c, pl.ds(s, 1), : z.main] for c in range(3)] for s in slots]
        for h in range(2):
            hats.append(hat_tables(z, *lines[h], plane_ref, h * z.main))
        picked = jnp.dot(
            flow_ref[...], plane_ref[:, : 2 * z.main], preferred_element_type=F32
        )
        for h in range(2):
            for c in range(3):
                part = picked[
                    c * z.width_x : (c + 1) * z.width_x, h * z.main : (h + 1) * z.main
                ]
                drift = jnp.sum(part * hats[h], axis=0, keepdims=True)
                places_ref[c, pl.ds(slots[h], 1), : z.main] = lines[h][c] + drift
        return carry

    lax.fori_loop(0, pairs, step, 0)


def sample_tails(z, places_ref, flow_ref, plane_ref):
    line = [tails_to_lanes(z, places_ref, c) for c in range(3)]
    hat_x = hat_tables(z, *line, plane_ref, 0)
    picked = jnp.dot(flow_ref[...], plane_ref[:, :LANES], preferred_element_type=F32)
    rows = places_ref.shape[1]
    lane = lane_index((rows, LANES))
    row = row_index((rows, LANES))
    for c in range(3):
        drift = jnp.sum(picked[c * z.width_x : (c + 1) * z.width_x] * hat_x, axis=0, keepdims=True)
        ends = places_ref[c, :, z.main :]
        for t in range(z.tail):
            moved = jnp.sum(
                jnp.where(lane == row * z.tail + t, drift, 0.0), axis=1, keepdims=True
            )
            ends = jnp.where(lane == t, ends + moved, ends)
        places_ref[c, :, z.main :] = ends


def collide(z, flow_ref, grid_ref, post_ref):
    def block(r, carry):
        rows = pl.ds(pl.multiple_of(r * 8, 8), 8)
        for t in range(z.plane // LANES):
            lanes = slice(t * LANES, (t + 1) * LANES)
            f = [flow_ref[q, rows, lanes] for q in range(19)]
            push = [
                PUSH_SCALE
                * grid_ref[pl.ds(pl.multiple_of(c * z.width_x + r * 8, 8), 8), lanes]
                for c in range(3)
            ]
            density = f[0]
            for q in range(1, 19):
                density = density + f[q]
            inverse = 1.0 / density
            u = []
            for c in range(3):
                m = 0.5 * push[c]
                for q in range(1, 19):
                    v = LATTICE_VELOCITY[q][c]
                    if v == 1:
                        m = m + f[q]
                    elif v == -1:
                        m = m - f[q]
                u.append(m * inverse)
            square = u[0] * u[0] + u[1] * u[1] + u[2] * u[2]
            work = u[0] * push[0] + u[1] * push[1] + u[2] * push[2]
            gain = 1.0 - 0.5 * RELAX_RATE
            heavy = RELAX_RATE * density
            base = heavy * (1.0 - 1.5 * square) - (3.0 * gain) * work
            post_ref[0, rows, lanes] = (1.0 - RELAX_RATE) * f[0] + LATTICE_WEIGHT[0] * base
            for q in range(1, 19, 2):
                along = None
                pull = None
                for c in range(3):
                    v = LATTICE_VELOCITY[q][c]
                    if v:
                        along = v * u[c] if along is None else along + v * u[c]
                        pull = v * push[c] if pull is None else pull + v * push[c]
                w = LATTICE_WEIGHT[q]
                lifted = heavy * along
                even = w * (base + along * (4.5 * lifted + (9.0 * gain) * pull))
                odd = (3.0 * w) * (lifted + gain * pull)
                post_ref[q, rows, lanes] = (1.0 - RELAX_RATE) * f[q] + (even + odd)
                post_ref[q + 1, rows, lanes] = (1.0 - RELAX_RATE) * f[q + 1] + (even - odd)
        return carry

    lax.fori_loop(0, z.width_x // 8, block, 0)


def write_edges(z, post_ref, right_ref, left_ref, up_ref, down_ref):
    for number, q in enumerate(RIGHT_MOVERS):
        right_ref[number : number + 1, :] = post_ref[q, z.width_x - 1 : z.width_x, :]
    for number, q in enumerate(LEFT_MOVERS):
        left_ref[number : number + 1, :] = post_ref[q, 0:1, :]
    right_ref[5:8, :] = jnp.zeros((3, z.plane), F32)
    left_ref[5:8, :] = jnp.zeros((3, z.plane), F32)
    lane = lane_index((z.width_x, LANES))
    up = jnp.zeros((z.width_x, LANES), F32)
    down = jnp.zeros((z.width_x, LANES), F32)
    for number, q in enumerate(UPWARD_MOVERS):
        here = (lane >= number * CZ) & (lane < (number + 1) * CZ)
        value = post_ref[q, :, z.plane - LANES :]
        up = jnp.where(here, pltpu.roll(value, (number + 1) * CZ, 1), up)
    for number, q in enumerate(DOWNWARD_MOVERS):
        here = (lane >= number * CZ) & (lane < (number + 1) * CZ)
        value = post_ref[q, :, :LANES]
        down = jnp.where(here, value if number == 0 else pltpu.roll(value, number * CZ, 1), down)
    up_ref[...] = up
    down_ref[...] = down


def stream(z, post_ref, from_left_ref, from_right_ref, below_ref, above_ref, out_ref, grid_ref, flow_ref):
    shape = (z.width_x, z.plane)
    lane = lane_index(shape)
    row = row_index(shape)
    edge_row = row_index((z.width_x, LANES))
    layer = lax.rem(lane, CZ)
    last_row = z.width_x - 1
    sums = [None] * 4
    for q in range(19):
        cx, cy, cz = LATTICE_VELOCITY[q]
        value = post_ref[q]
        if cx == 1:
            k = RIGHT_MOVERS.index(q)
            value = jnp.where(row == 0, from_left_ref[k : k + 1, :], pltpu.roll(value, 1, 0))
        elif cx == -1:
            k = LEFT_MOVERS.index(q)
            value = jnp.where(
                row == last_row, from_right_ref[k : k + 1, :], pltpu.roll(value, last_row, 0)
            )
        if cy:
            edges = below_ref if cy == 1 else above_ref
            k = (UPWARD_MOVERS if cy == 1 else DOWNWARD_MOVERS).index(q)
            edge = edges[: z.width_x, :]
            shift = (LANES - k * CZ if cy == 1 else 2 * LANES - (k + 1) * CZ) % LANES
            edge = edge if shift == 0 else pltpu.roll(edge, shift, 1)
            if cx:
                movers = RIGHT_MOVERS if cx == 1 else LEFT_MOVERS
                at = z.width_x + (0 if cx == 1 else 8) + movers.index(q)
                corner = edges[at : at + 1, :]
                turn = CZ if cy == 1 else LANES - CZ
                corner = pltpu.roll(corner, turn, 1)
                if cx == 1:
                    edge = jnp.where(edge_row == 0, corner, pltpu.roll(edge, 1, 0))
                else:
                    edge = jnp.where(edge_row == last_row, corner, pltpu.roll(edge, last_row, 0))
            rest = jnp.zeros((z.width_x, z.plane - LANES), F32)
            if cy == 1:
                wide = jnp.concatenate([edge, rest], axis=1)
                value = jnp.where(lane < CZ, wide, pltpu.roll(value, CZ, 1))
            else:
                wide = jnp.concatenate([rest, edge], axis=1)
                value = jnp.where(lane >= z.plane - CZ, wide, pltpu.roll(value, z.plane - CZ, 1))
        if cz == 1:
            value = jnp.where(
                layer == 0, pltpu.roll(value, z.plane - (CZ - 1), 1), pltpu.roll(value, 1, 1)
            )
        elif cz == -1:
            value = jnp.where(
                layer == CZ - 1, pltpu.roll(value, CZ - 1, 1), pltpu.roll(value, z.plane - 1, 1)
            )
        out_ref[q] = value
    for r in range(z.width_x // 8):
        rows = slice(r * 8, (r + 1) * 8)
        for t in range(z.plane // LANES):
            lanes = slice(t * LANES, (t + 1) * LANES)
            f = [out_ref[q, rows, lanes] for q in range(19)]
            density = f[0]
            for q in range(1, 19):
                density = density + f[q]
            inverse = 1.0 / density
            for c in range(3):
                m = (0.5 * PUSH_SCALE) * grid_ref[
                    c * z.width_x + r * 8 : c * z.width_x + (r + 1) * 8, lanes
                ]
                for q in range(1, 19):
                    v = LATTICE_VELOCITY[q][c]
                    if v == 1:
                        m = m + f[q]
                    elif v == -1:
                        m = m - f[q]
                sums[c] = m * inverse
            for c in range(3):
                flow_ref[c * z.width_x + r * 8 : c * z.width_x + (r + 1) * 8, lanes] = sums[c]


IDS = 128


def layout(z):
    return (0, 2), (1, 2 + z.center)


def read_flags(z, refs, flags_ref, sem):
    copies = []
    for g, (ref, at) in enumerate(refs):
        view = ref if at is None else ref.at[at]
        copies.append(
            pltpu.make_async_copy(
                view.at[:, pl.ds(3 * z.main, LANES)], flags_ref.at[g], sem.at[g]
            )
        )
    return copies


def center_kernel(z, *refs):
    d = z.devices_y
    center = refs[:d]
    shape_ref, link_ref, degree_ref, grid_ref = refs[d : d + 4]
    places, ends, stiff, force, plane, lift, flags, ids, sem = refs[d + 4 :]
    copies = read_flags(z, [(r, None) for r in center], flags, sem)
    for copy in copies:
        copy.start()
    for e in range(d):
        split_message(z, center[e], None, places, ends, e * CAP)
    place_tails(z, ends, places, stiff)
    forces(z, places, stiff, shape_ref, link_ref, degree_ref, force)
    grid_ref[...] = jnp.zeros_like(grid_ref)
    for copy in copies:
        copy.wait()
    (count_at, start), _ = layout(z)
    list_active(
        lambda s: flags[lax.div(s, CAP), lax.rem(s, CAP), 3 * z.tail], 0, z.center, ids, start, count_at
    )
    spread(z, places, force, ids, start, ids[count_at], grid_ref, plane, lift, True)


def sides_kernel(z, *refs):
    d = z.devices_y
    center, sides = refs[:d], refs[d : 2 * d]
    shape_ref, link_ref, degree_ref, part_ref, flow_ref = refs[2 * d : 2 * d + 5]
    (
        grid_ref,
        post_ref,
        right_ref,
        left_ref,
        up_ref,
        down_ref,
        places_ref,
        stiff_ref,
        ids_ref,
    ) = refs[2 * d + 5 : 2 * d + 14]
    ends, side_places, side_ends, side_stiff, force, plane, lift, flags, sem = refs[2 * d + 14 :]
    sources = [(r, None) for r in center]
    for e in range(d):
        sources += [(sides[e], 0), (sides[e], 1)]
    copies = read_flags(z, sources, flags, sem)
    for copy in copies:
        copy.start()
    for g, (ref, at) in enumerate(sources):
        split_message(z, ref, at, places_ref, ends, g * CAP)
        if g >= d:
            split_message(z, ref, at, side_places, side_ends, (g - d) * CAP)
    place_tails(z, ends, places_ref, stiff_ref)
    place_tails(z, side_ends, side_places, side_stiff)
    forces(z, side_places, side_stiff, shape_ref, link_ref, degree_ref, force)
    grid_ref[...] = part_ref[...]
    for copy in copies:
        copy.wait()
    flag = lambda s: flags[lax.div(s, CAP), lax.rem(s, CAP), 3 * z.tail]
    (center_count, center_start), (side_count, side_start) = layout(z)
    list_active(flag, 0, z.center, ids_ref, center_start, center_count)
    list_active(
        lambda s: flag(s + z.center), 0, z.slots - z.center, ids_ref, side_start, side_count
    )
    spread(z, side_places, force, ids_ref, side_start, ids_ref[side_count], grid_ref, plane, lift, True)
    collide(z, flow_ref, grid_ref, post_ref)
    write_edges(z, post_ref, right_ref, left_ref, up_ref, down_ref)


def copy_ids(z, ids_ref, out_ref):
    (center_count, center_start), (side_count, side_start) = layout(z)
    out_ref[center_count] = ids_ref[center_count]
    out_ref[side_count] = ids_ref[side_count]

    def one(i, carry):
        out_ref[center_start + i] = ids_ref[center_start + i]
        return carry

    def other(i, carry):
        out_ref[side_start + i] = ids_ref[side_start + i] + z.center
        return carry

    lax.fori_loop(0, 2 * ids_ref[center_count], one, 0)
    lax.fori_loop(0, 2 * ids_ref[side_count], other, 0)


def middle_kernel(z, *refs):
    (
        post_ref,
        from_left,
        from_right,
        below,
        above,
        old_grid,
        old_places,
        stiff_ref,
        ids_ref,
        shape_ref,
        link_ref,
        degree_ref,
    ) = refs[:12]
    grid_ref, next_ref, right_ref, left_ref, up_ref, down_ref, places_ref = refs[12:19]
    moved, flow32, flow, force, plane, lift, ids = refs[19:]
    copy_ids(z, ids_ref, ids)
    places_ref[...] = old_places[...]
    stream(z, post_ref, from_left, from_right, below, above, moved, old_grid, flow32)
    flow[...] = flow32[...].astype(BF16)
    grid_ref[...] = jnp.zeros_like(grid_ref)
    lists = layout(z)
    sample_tails(z, places_ref, flow, plane)
    for count_at, start in lists:
        sample(z, places_ref, flow, ids, start, ids[count_at], plane)
    forces(z, places_ref, stiff_ref, shape_ref, link_ref, degree_ref, force)
    for number, (count_at, start) in enumerate(lists):
        spread(
            z, places_ref, force, ids, start, ids[count_at], grid_ref, plane, lift, number == 0
        )
    collide(z, moved, grid_ref, next_ref)
    write_edges(z, next_ref, right_ref, left_ref, up_ref, down_ref)


def join_message(z, places_ref, slot, out_ref, at):
    lane = lane_index((CAP, LANES))
    ends = jnp.zeros((CAP, LANES), F32)
    for c in range(3):
        line = places_ref[c, slot : slot + CAP, :]
        lanes = slice(c * z.main, (c + 1) * z.main)
        if at is None:
            out_ref[:, lanes] = line[:, : z.main]
        else:
            out_ref[at, :, lanes] = line[:, : z.main]
        end = jnp.where(lane < z.tail, line[:, z.main :], 0.0)
        ends = ends + (end if c == 0 else pltpu.roll(end, c * z.tail, 1))
    if at is None:
        out_ref[:, 3 * z.main :] = ends
    else:
        out_ref[at, :, 3 * z.main :] = ends


def last_sides_kernel(z, *refs):
    d = z.devices_y
    (post_ref, from_left, from_right, below, above, grid_ref, old_places, ids_ref) = refs[:8]
    moved_ref, flow_ref, tail_places_ref = refs[8:11]
    side_refs = refs[11 : 11 + d]
    flow32, places, plane, ids = refs[11 + d :]
    copy_ids(z, ids_ref, ids)
    places[...] = old_places[...]
    stream(z, post_ref, from_left, from_right, below, above, moved_ref, grid_ref, flow32)
    flow_ref[...] = flow32[...].astype(BF16)
    sample_tails(z, places, flow_ref, plane)
    _, (count_at, start) = layout(z)
    sample(z, places, flow_ref, ids, start, ids[count_at], plane)
    for e in range(d):
        for h in range(2):
            join_message(z, places, z.center + (2 * e + h) * CAP, side_refs[e], h)
    tail_places_ref[...] = places[:, : z.center, :]


def last_center_kernel(z, *refs):
    d = z.devices_y
    flow_ref, old_places, ids_ref = refs[:3]
    center_refs = refs[3 : 3 + d]
    places, plane = refs[3 + d :]
    places[...] = old_places[...]
    (count_at, start), _ = layout(z)
    sample(z, places, flow_ref, ids_ref, start, ids_ref[count_at], plane)
    for e in range(d):
        join_message(z, places, e * CAP, center_refs[e], None)


def shift(value, axis, step):
    count = lax.axis_size(axis)
    return lax.ppermute(value, axis, [(i, (i + step) % count) for i in range(count)])


def trade_edges(z, right, left, up, down):
    from_left = shift(right, "gx", 1)
    from_right = shift(left, "gx", -1)
    far, near = slice(z.plane - LANES, z.plane), slice(0, LANES)
    up = jnp.concatenate([up, from_left[:, far], from_right[:, far]], axis=0)
    down = jnp.concatenate([down, from_left[:, near], from_right[:, near]], axis=0)
    return from_left, from_right, shift(up, "gy", 1), shift(down, "gy", -1)


def local(populations, positions, stiffness, membrane_shape, neighbours, home_tile):
    z = Sizes(
        positions.shape[0],
        positions.shape[2],
        populations.shape[1],
        populations.shape[2],
        lax.axis_size("gx"),
        lax.axis_size("gy"),
    )
    d = z.devices_y
    run = functools.partial
    line = (CAP, z.message)
    table = VMEM((3 * d,) + line, F32)
    counts = SMEM((3 * d,), jnp.int32)
    packed = call(
        run(pack_kernel, z),
        [((d,) + line, F32, VMEM)] * 2 + [(line, F32, VMEM)] * d,
        [SMEM, SMEM, VMEM],
        [table, counts],
    )(home_tile, stiffness, positions)
    to_left, to_right, center = packed[0], packed[1], packed[2:]
    from_left = shift(to_right, "gx", 1)
    from_right = shift(to_left, "gx", -1)
    center = [center[0]] + [shift(center[e], "gy", e) for e in range(1, d)]
    pad = z.full - z.vertices
    near = jnp.pad(neighbours, ((0, pad), (0, 0)), constant_values=-1)
    shape = jnp.pad(membrane_shape, ((0, 0), (0, pad)))
    link, degree = call(
        run(matrix_kernel, z),
        [((z.full, z.full), BF16, VMEM), ((1, z.full), F32, VMEM)],
        [VMEM, VMEM],
    )(near, near.T)
    sides = [jnp.stack([from_left[e], from_right[e]]) for e in range(d)]
    sides = [sides[0]] + [shift(sides[e], "gy", e) for e in range(1, d)]

    grid_type = ((3 * z.width_x, z.plane), F32, VMEM)
    post_type = ((19, z.width_x, z.plane), F32, VMEM)
    plane_scratch = VMEM((z.plane, 2 * z.main), BF16)
    lift_scratch = VMEM((3 * z.width_x, 2 * z.main), BF16)
    edge_types = [((8, z.plane), F32, VMEM)] * 2 + [((z.width_x, LANES), F32, VMEM)] * 2

    def rows(n):
        return VMEM((3, n, z.full), F32)

    def ends(n):
        return VMEM((n, LANES), F32)

    (part,) = call(
        run(center_kernel, z),
        [grid_type],
        [VMEM] * (d + 3),
        [
            rows(z.center),
            ends(z.center),
            ends(z.center),
            rows(z.center),
            plane_scratch,
            lift_scratch,
            SMEM((d, CAP, LANES), F32),
            SMEM((IDS,), jnp.int32),
            pltpu.SemaphoreType.DMA((d,)),
        ],
        pl.CostEstimate(flops=2_000_000_000, bytes_accessed=4_000_000, transcendentals=0),
    )(*center, shape, link, degree)
    n_sides = z.slots - z.center
    places_type = ((3, z.slots, z.full), F32, VMEM)
    grid, post, right, left, up, down, places, stiff, ids = call(
        run(sides_kernel, z),
        [grid_type, post_type]
        + edge_types
        + [places_type, ((z.slots, LANES), F32, VMEM), ((IDS,), jnp.int32, SMEM)],
        [VMEM] * (2 * d + 5),
        [
            ends(z.slots),
            rows(n_sides),
            ends(n_sides),
            ends(n_sides),
            rows(n_sides),
            plane_scratch,
            lift_scratch,
            SMEM((3 * d, CAP, LANES), F32),
            pltpu.SemaphoreType.DMA((3 * d,)),
        ],
    )(*center, *sides, shape, link, degree, part, populations)
    for _ in range(STEPS - 1):
        edges = trade_edges(z, right, left, up, down)
        grid, post, right, left, up, down, places = call(
            run(middle_kernel, z),
            [grid_type, post_type] + edge_types + [places_type],
            [VMEM] * 8 + [SMEM] + [VMEM] * 3,
            [
                VMEM(post_type[0], F32),
                VMEM(grid_type[0], F32),
                VMEM(grid_type[0], BF16),
                rows(z.slots),
                plane_scratch,
                lift_scratch,
                SMEM((IDS,), jnp.int32),
            ],
        )(post, *edges, grid, places, stiff, ids, shape, link, degree)
    edges = trade_edges(z, right, left, up, down)
    last = call(
        run(last_sides_kernel, z),
        [post_type, (grid_type[0], BF16, VMEM), ((3, z.center, z.full), F32, VMEM)]
        + [((2,) + line, F32, VMEM)] * d,
        [VMEM] * 7 + [SMEM],
        [VMEM(grid_type[0], F32), rows(z.slots), plane_scratch, SMEM((IDS,), jnp.int32)],
    )(post, *edges, grid, places, ids)
    moved, flow, center_places, sides = last[0], last[1], last[2], last[3:]
    sides = [sides[0]] + [shift(sides[e], "gy", -e) for e in range(1, d)]
    center = call(
        run(last_center_kernel, z),
        [(line, F32, VMEM)] * d,
        [VMEM, VMEM, SMEM],
        [rows(z.center), plane_scratch],
        pl.CostEstimate(flops=2_000_000_000, bytes_accessed=4_000_000, transcendentals=0),
    )(flow, center_places, ids)
    center = [center[0]] + [shift(center[e], "gy", -e) for e in range(1, d)]
    to_left = jnp.stack([sides[e][0] for e in range(d)])
    to_right = jnp.stack([sides[e][1] for e in range(d)])
    right_part = shift(to_left, "gx", -1)
    left_part = shift(to_right, "gx", 1)
    (displacement,) = call(
        run(unpack_kernel, z),
        [(positions.shape, F32, VMEM)],
        [SMEM] + [VMEM] * (3 + d),
        [table, counts],
    )(home_tile, positions, left_part, right_part, *center)
    return moved, displacement, grid.reshape(3, z.width_x, z.plane)


def solution(mesh):
    placed = (
        P(None, "gx", "gy"),
        P(("gx", "gy"), None, None),
        P(("gx", "gy")),
        P(),
        P(),
        P(("gx", "gy")),
    )
    return jax.shard_map(
        local,
        mesh=mesh,
        in_specs=placed,
        out_specs=(P(None, "gx", "gy"), P(("gx", "gy"), None, None), P(None, "gx", "gy")),
        check_vma=False,
    )
```

```python
import functools

import jax
import jax.numpy as jnp
from jax import lax
from jax.experimental import pallas as pl
from jax.experimental.pallas import tpu as pltpu
from jax.sharding import PartitionSpec as P

CZ = 16
CAP = 4
STEPS = 2

LATTICE_VELOCITY = [
    [0, 0, 0],
    [1, 0, 0],
    [-1, 0, 0],
    [0, 1, 0],
    [0, -1, 0],
    [0, 0, 1],
    [0, 0, -1],
    [1, 1, 0],
    [-1, -1, 0],
    [1, -1, 0],
    [-1, 1, 0],
    [1, 0, 1],
    [-1, 0, -1],
    [1, 0, -1],
    [-1, 0, 1],
    [0, 1, 1],
    [0, -1, -1],
    [0, 1, -1],
    [0, -1, 1],
]
LATTICE_WEIGHT = [1.0 / 3.0] + [1.0 / 18.0] * 6 + [1.0 / 36.0] * 12
RIGHT_MOVERS = [1, 7, 9, 11, 13]
LEFT_MOVERS = [2, 8, 10, 12, 14]
UPWARD_MOVERS = [3, 7, 10, 15, 17]
DOWNWARD_MOVERS = [4, 8, 9, 16, 18]
RELAX_RATE = 1.25
PUSH_SCALE = 0.05
TETHER_GAIN = 2.0
LANES = 128
WINDOW = 16
SLOW = 15
FAST_AT = 2
SLOW_AT = 64
CODE_AT = 128
LISTS = 256
F32 = jnp.float32
BF16 = jnp.bfloat16
SMEM = pltpu.SMEM
VMEM = pltpu.VMEM


def spec(space):
    return pl.BlockSpec(memory_space=space)


def call(kernel, outs, ins, scratch=(), cost=None, limit=None):
    return pl.pallas_call(
        kernel,
        out_shape=[jax.ShapeDtypeStruct(s, d) for s, d, _ in outs],
        in_specs=[spec(m) for m in ins],
        out_specs=[spec(m) for _, _, m in outs],
        scratch_shapes=list(scratch),
        compiler_params=pltpu.CompilerParams(vmem_limit_bytes=limit or (24 << 20)),
        cost_estimate=cost,
    )


def lane_index(shape):
    return lax.broadcasted_iota(jnp.int32, shape, len(shape) - 1)


def row_index(shape):
    return lax.broadcasted_iota(jnp.int32, shape, len(shape) - 2)


class Sizes:
    def __init__(self, cells, vertices, width_x, plane, devices_x, devices_y):
        self.cells = cells
        self.vertices = vertices
        self.width_x = width_x
        self.plane = plane
        self.devices_x = devices_x
        self.devices_y = devices_y
        self.main = vertices - vertices % LANES
        self.tail = vertices - self.main
        self.full = self.main + LANES
        self.message = 3 * self.main + LANES
        self.groups = 3 * devices_y
        self.slots = 3 * devices_y * CAP
        self.width_y = plane // CZ


def cell_places(z, home_ref, count_ref):
    own_x = lax.axis_index("gx")
    own_y = lax.axis_index("gy")
    for g in range(z.groups):
        count_ref[g] = 0
    found = []
    for n in range(z.cells):
        home = home_ref[n]
        target_x = lax.div(home, z.devices_y)
        target_y = lax.rem(home, z.devices_y)
        side = lax.rem(target_x - own_x + 1 + z.devices_x, z.devices_x)
        turn = lax.rem(target_y - own_y + z.devices_y, z.devices_y)
        group = side * z.devices_y + turn
        rank = count_ref[group]
        count_ref[group] = rank + 1
        found.append((group, rank))
    return found


def pack_kernel(z, home_ref, stiff_ref, places_ref, left_ref, center_ref, right_ref, table_ref, count_ref):
    table_ref[...] = jnp.zeros_like(table_ref)
    lane = lane_index((1, LANES))
    zeros = jnp.zeros((1, LANES - z.tail), F32)
    for n, (group, rank) in enumerate(cell_places(z, home_ref, count_ref)):
        ends = jnp.where(lane == 3 * z.tail, stiff_ref[n], 0.0)
        parts = []
        for c in range(3):
            line = places_ref[c, n : n + 1, :]
            parts.append(line[:, : z.main])
            end = jnp.concatenate([line[:, z.main :], zeros], axis=1)
            ends = ends + (end if c == 0 else pltpu.roll(end, c * z.tail, 1))
        table_ref[group, pl.ds(rank, 1), :] = jnp.concatenate(parts + [ends], axis=1)
    d = z.devices_y
    left_ref[...] = table_ref[0:d]
    center_ref[...] = table_ref[d : 2 * d]
    right_ref[...] = table_ref[2 * d : 3 * d]


def unpack_kernel(z, home_ref, places_ref, left_ref, right_ref, *rest):
    center_refs = rest[: z.devices_y]
    out_ref, table_ref, count_ref = rest[z.devices_y :]
    d = z.devices_y
    table_ref[0:d] = left_ref[...]
    table_ref[2 * d : 3 * d] = right_ref[...]
    for r in range(d):
        table_ref[d + r] = center_refs[r][0]
    for n, (group, rank) in enumerate(cell_places(z, home_ref, count_ref)):
        line = table_ref[group, pl.ds(rank, 1), :]
        ends = line[:, 3 * z.main :]
        for c in range(3):
            end = ends if c == 0 else pltpu.roll(ends, LANES - c * z.tail, 1)
            whole = jnp.concatenate([line[:, c * z.main : (c + 1) * z.main], end], axis=1)
            out_ref[c, n : n + 1, :] = whole[:, : z.vertices] - places_ref[c, n : n + 1, :]


def matrix_kernel(z, near_ref, shape_ref, link_ref, degree_ref, rest_ref, half_ref):
    near = near_ref[...]
    shape = shape_ref[...]
    rest_ref[...] = jnp.concatenate(
        [shape, jnp.zeros((3, z.full - z.vertices), F32)], axis=1
    )
    entries = near.shape[0]
    tiles = z.full // LANES
    missing = jnp.full((entries, z.full - z.vertices), -1, jnp.int32)
    near = jnp.concatenate([near, missing], axis=1)
    row = row_index((LANES, LANES))
    for t in range(tiles):
        lines = near[:, t * LANES : (t + 1) * LANES]
        for r in range(tiles):
            total = jnp.zeros((LANES, LANES), F32)
            for b in range(entries):
                total += jnp.where(lines[b : b + 1] == row + r * LANES, 1.0, 0.0)
            half_ref[r * LANES : (r + 1) * LANES, t * LANES : (t + 1) * LANES] = total
    for t in range(tiles):
        lanes = slice(t * LANES, (t + 1) * LANES)
        degree = jnp.zeros((1, LANES), F32) + TETHER_GAIN
        for r in range(tiles):
            rows = slice(r * LANES, (r + 1) * LANES)
            total = half_ref[rows, lanes] + half_ref[lanes, rows].T
            link_ref[rows, lanes] = total.astype(BF16)
            degree += jnp.sum(total, axis=0, keepdims=True)
        degree_ref[:, lanes] = degree


def split_message(z, value, places_ref, ends_ref, slot):
    for c in range(3):
        places_ref[c, slot : slot + CAP, : z.main] = value[:, c * z.main : (c + 1) * z.main]
    ends_ref[slot : slot + CAP, :] = value[:, 3 * z.main :]


def place_tails(z, ends_ref, places_ref, stiff_ref):
    ends = ends_ref[...]
    lane = lane_index(ends.shape)
    for c in range(3):
        end = ends if c == 0 else pltpu.roll(ends, LANES - c * z.tail, 1)
        places_ref[c, :, z.main :] = jnp.where(lane < z.tail, end, 0.0)
    stiff_ref[...] = jnp.broadcast_to(ends[:, 3 * z.tail : 3 * z.tail + 1], ends.shape)


def forces(z, places_ref, stiff_ref, shape_ref, link_ref, degree_ref, force_ref):
    rows = places_ref.shape[1]
    lane = lane_index((rows, z.full))
    inside = lane < z.vertices
    parts = []
    for c in range(3):
        x = places_ref[c]
        mean = jnp.sum(x, axis=1, keepdims=True) * (1.0 / z.vertices)
        parts.append(jnp.where(inside, x - mean - shape_ref[c : c + 1, :], 0.0))
    strain = jnp.concatenate(parts, axis=0)
    high = strain.astype(BF16)
    rest = strain - high.astype(F32)
    low = rest.astype(BF16)
    link = link_ref[...]
    linked = jnp.dot(high, link, preferred_element_type=F32) + jnp.dot(
        low, link, preferred_element_type=F32
    )
    pulled = degree_ref[...] * (high.astype(F32) + low.astype(F32)) - linked
    stiff = stiff_ref[:, 0:1]
    for c in range(3):
        force_ref[c] = -stiff * pulled[c * rows : (c + 1) * rows]


def list_slots(z, places_ref, stiff_ref, lists_ref):
    codes = None
    fits = None
    for c, width in ((0, z.width_x), (1, z.width_y)):
        x = places_ref[c, :, : z.main]
        low = jnp.maximum(jnp.floor(jnp.min(x, axis=1, keepdims=True)), 0.0)
        high = jnp.minimum(jnp.floor(jnp.max(x, axis=1, keepdims=True)) + 1.0, width - 1.0)
        block = jnp.minimum(jnp.floor(low * 0.125), (width - WINDOW) // 8 * 1.0)
        fit = high - 8.0 * block <= WINDOW - 1.0
        codes = block if codes is None else codes + 4.0 * block
        fits = fit if fits is None else fits & fit
    codes = jnp.where(fits, codes, SLOW * 1.0)
    codes = jnp.where(stiff_ref[:, 0:1] > 0.0, codes, -1.0).astype(jnp.int32)
    for s in range(z.slots):
        lists_ref[CODE_AT + s] = codes[s, 0]

    def step(s, state):
        fast, slow, empty = state
        code = lists_ref[CODE_AT + s]
        is_slow = code == SLOW
        is_fast = (code >= 0) & (code < SLOW)

        @pl.when(is_fast)
        def _():
            lists_ref[FAST_AT + fast] = s

        @pl.when(is_slow)
        def _():
            lists_ref[SLOW_AT + slow] = s

        @pl.when(code < 0)
        def _():
            lists_ref[CODE_AT + s] = 0

        return (
            jnp.where(is_fast, fast + 1, fast),
            jnp.where(is_slow, slow + 1, slow),
            jnp.where(code < 0, s, empty),
        )

    zero = jnp.int32(0)
    fast, slow, empty = lax.fori_loop(0, z.slots, step, (zero, zero, zero))

    @pl.when(lax.rem(fast, 2) == 1)
    def _():
        lists_ref[FAST_AT + fast] = empty

    @pl.when(lax.rem(slow, 2) == 1)
    def _():
        lists_ref[SLOW_AT + slow] = empty

    lists_ref[0] = lax.div(fast + 1, 2)
    lists_ref[1] = lax.div(slow + 1, 2)


def window_of(lists_ref, s):
    code = lists_ref[CODE_AT + s]
    return 8 * lax.rem(code, 4), 8 * lax.div(code, 4)


def tails_to_lanes(z, ref, c):
    ends = ref[c, :, z.main :]
    lane = lane_index(ends.shape)
    row = row_index(ends.shape)
    picked = jnp.zeros_like(ends)
    for t in range(z.tail):
        picked = jnp.where(lane == row * z.tail + t, ends[:, t : t + 1], picked)
    return jnp.sum(picked, axis=0, keepdims=True)


def hat_tables(x, y, depth, first_x, count_x, first_y, count_y, plane_ref, rows_at, at):
    width = x.shape[1]
    steps_x = row_index((count_x, width)).astype(F32)
    steps_y = row_index((count_y, width)).astype(F32)
    if first_x is not None:
        steps_x = steps_x + first_x
        steps_y = steps_y + first_y
    steps_z = row_index((CZ, width)).astype(F32)
    hat_x = jnp.maximum(0.0, 1.0 - jnp.abs(x - steps_x))
    hat_y = jnp.maximum(0.0, 1.0 - jnp.abs(y - steps_y))
    wrapped = depth - CZ * jnp.floor(depth * (1.0 / CZ))
    gap = jnp.abs(wrapped - steps_z)
    hat_z = jnp.maximum(0.0, 1.0 - jnp.minimum(gap, CZ - gap))
    for j in range(count_y):
        rows = slice(rows_at + j * CZ, rows_at + (j + 1) * CZ)
        plane_ref[rows, at : at + width] = (hat_y[j : j + 1] * hat_z).astype(BF16)
    return hat_x


def contract(lift, plane):
    return lax.dot_general(lift, plane, (((1,), (1,)), ((), ())), preferred_element_type=F32)


def spread(z, places_ref, force_ref, lists_ref, grid_ref, plane_ref, lift_ref):
    grid_ref[...] = jnp.zeros_like(grid_ref)

    def fill(line, pull, firsts, counts, at, plane_row, lift_row):
        hat_x = hat_tables(*line, firsts[0], counts[0], firsts[1], counts[1], plane_ref, plane_row, at)
        width = line[0].shape[1]
        for c in range(3):
            row = lift_row + c * counts[0]
            lift_ref[row : row + counts[0], at : at + width] = (pull[c] * hat_x).astype(BF16)

    def load(s):
        line = [places_ref[c, pl.ds(s, 1), : z.main] for c in range(3)]
        pull = [force_ref[c, pl.ds(s, 1), : z.main] for c in range(3)]
        return line, pull

    whole = (z.width_x, z.width_y)
    window = (WINDOW, WINDOW)
    plane_rows = WINDOW * CZ
    lift_rows = 3 * WINDOW

    def fast(p, carry):
        firsts = []
        for h in range(2):
            s = lists_ref[FAST_AT + 2 * p + h]
            first = window_of(lists_ref, s)
            firsts.append(first)
            line, pull = load(s)
            fill(
                line, pull, [f.astype(F32) for f in first], window, 0, h * plane_rows, h * lift_rows
            )
        for h in range(2):
            part = contract(
                lift_ref[h * lift_rows : (h + 1) * lift_rows, : z.main],
                plane_ref[h * plane_rows : (h + 1) * plane_rows, : z.main],
            )
            lanes = pl.ds(pl.multiple_of(firsts[h][1] * CZ, LANES), plane_rows)
            for c in range(3):
                rows = pl.ds(pl.multiple_of(c * z.width_x + firsts[h][0], 8), WINDOW)
                grid_ref[rows, lanes] += part[c * WINDOW : (c + 1) * WINDOW]
        return carry

    def slow(p, carry):
        for h in range(2):
            line, pull = load(lists_ref[SLOW_AT + 2 * p + h])
            fill(line, pull, (None, None), whole, h * z.main, 0, 0)
        grid_ref[...] += contract(lift_ref[...], plane_ref[...])
        return carry

    line = [tails_to_lanes(z, places_ref, c) for c in range(3)]
    pull = [tails_to_lanes(z, force_ref, c) for c in range(3)]
    fill(line, pull, (None, None), whole, 0, 0, 0)
    grid_ref[...] = contract(lift_ref[:, :LANES], plane_ref[:, :LANES])
    lax.fori_loop(0, lists_ref[0], fast, 0)
    lax.fori_loop(0, lists_ref[1], slow, 0)


def sample(z, places_ref, flow_ref, lists_ref, plane_ref):
    plane_rows = WINDOW * CZ

    def load(s):
        return [places_ref[c, pl.ds(s, 1), : z.main] for c in range(3)]

    def move(s, line, picked, hat_x, count_x):
        for c in range(3):
            drift = jnp.sum(picked[c * count_x : (c + 1) * count_x] * hat_x, axis=0, keepdims=True)
            places_ref[c, pl.ds(s, 1), : z.main] = line[c] + drift

    def fast(p, carry):
        slots = [lists_ref[FAST_AT + 2 * p + h] for h in range(2)]
        firsts = [window_of(lists_ref, s) for s in slots]
        lines = [load(s) for s in slots]
        hats = [
            hat_tables(
                *lines[h],
                firsts[h][0].astype(F32),
                WINDOW,
                firsts[h][1].astype(F32),
                WINDOW,
                plane_ref,
                h * plane_rows,
                0,
            )
            for h in range(2)
        ]
        picked = []
        for h in range(2):
            lanes = pl.ds(pl.multiple_of(firsts[h][1] * CZ, LANES), plane_rows)
            flow = jnp.concatenate(
                [
                    flow_ref[
                        pl.ds(pl.multiple_of(c * z.width_x + firsts[h][0], 8), WINDOW), lanes
                    ]
                    for c in range(3)
                ],
                axis=0,
            ).astype(BF16)
            plane = plane_ref[h * plane_rows : (h + 1) * plane_rows, : z.main]
            picked.append(jnp.dot(flow, plane, preferred_element_type=F32))
        for h in range(2):
            move(slots[h], lines[h], picked[h], hats[h], WINDOW)
        return carry

    def slow(p, carry):
        slots = [lists_ref[SLOW_AT + 2 * p + h] for h in range(2)]
        lines = [load(s) for s in slots]
        hats = [
            hat_tables(
                *lines[h], None, z.width_x, None, z.width_y, plane_ref, 0, h * z.main
            )
            for h in range(2)
        ]
        picked = jnp.dot(
            flow_ref[...].astype(BF16), plane_ref[...], preferred_element_type=F32
        )
        for h in range(2):
            move(
                slots[h], lines[h], picked[:, h * z.main : (h + 1) * z.main], hats[h], z.width_x
            )
        return carry

    line = [tails_to_lanes(z, places_ref, c) for c in range(3)]
    hat_x = hat_tables(*line, None, z.width_x, None, z.width_y, plane_ref, 0, 0)
    picked = jnp.dot(
        flow_ref[...].astype(BF16), plane_ref[:, :LANES], preferred_element_type=F32
    )
    rows = places_ref.shape[1]
    lane = lane_index((rows, LANES))
    row = row_index((rows, LANES))
    for c in range(3):
        drift = jnp.sum(picked[c * z.width_x : (c + 1) * z.width_x] * hat_x, axis=0, keepdims=True)
        ends = places_ref[c, :, z.main :]
        for t in range(z.tail):
            moved = jnp.sum(
                jnp.where(lane == row * z.tail + t, drift, 0.0), axis=1, keepdims=True
            )
            ends = jnp.where(lane == t, ends + moved, ends)
        places_ref[c, :, z.main :] = ends
    lax.fori_loop(0, lists_ref[0], fast, 0)
    lax.fori_loop(0, lists_ref[1], slow, 0)


def collide(z, flow_ref, grid_ref, post_ref):
    def block(r, carry):
        rows = pl.ds(pl.multiple_of(r * 8, 8), 8)
        for t in range(z.plane // LANES):
            lanes = slice(t * LANES, (t + 1) * LANES)
            f = [flow_ref[q, rows, lanes] for q in range(19)]
            push = [
                PUSH_SCALE
                * grid_ref[pl.ds(pl.multiple_of(c * z.width_x + r * 8, 8), 8), lanes]
                for c in range(3)
            ]
            density = f[0]
            for q in range(1, 19):
                density = density + f[q]
            inverse = 1.0 / density
            u = []
            for c in range(3):
                m = 0.5 * push[c]
                for q in range(1, 19):
                    v = LATTICE_VELOCITY[q][c]
                    if v == 1:
                        m = m + f[q]
                    elif v == -1:
                        m = m - f[q]
                u.append(m * inverse)
            square = u[0] * u[0] + u[1] * u[1] + u[2] * u[2]
            work = u[0] * push[0] + u[1] * push[1] + u[2] * push[2]
            gain = 1.0 - 0.5 * RELAX_RATE
            heavy = RELAX_RATE * density
            base = heavy * (1.0 - 1.5 * square) - (3.0 * gain) * work
            post_ref[0, rows, lanes] = (1.0 - RELAX_RATE) * f[0] + LATTICE_WEIGHT[0] * base
            for q in range(1, 19, 2):
                along = None
                pull = None
                for c in range(3):
                    v = LATTICE_VELOCITY[q][c]
                    if v:
                        along = v * u[c] if along is None else along + v * u[c]
                        pull = v * push[c] if pull is None else pull + v * push[c]
                w = LATTICE_WEIGHT[q]
                lifted = heavy * along
                even = w * (base + along * (4.5 * lifted + (9.0 * gain) * pull))
                odd = (3.0 * w) * (lifted + gain * pull)
                post_ref[q, rows, lanes] = (1.0 - RELAX_RATE) * f[q] + (even + odd)
                post_ref[q + 1, rows, lanes] = (1.0 - RELAX_RATE) * f[q + 1] + (even - odd)
        return carry

    lax.fori_loop(0, z.width_x // 8, block, 0)


def write_edges(z, post_ref, right_ref, left_ref, up_ref, down_ref):
    for number, q in enumerate(RIGHT_MOVERS):
        right_ref[number : number + 1, :] = post_ref[q, z.width_x - 1 : z.width_x, :]
    for number, q in enumerate(LEFT_MOVERS):
        left_ref[number : number + 1, :] = post_ref[q, 0:1, :]
    right_ref[5:8, :] = jnp.zeros((3, z.plane), F32)
    left_ref[5:8, :] = jnp.zeros((3, z.plane), F32)
    lane = lane_index((z.width_x, LANES))
    up = jnp.zeros((z.width_x, LANES), F32)
    down = jnp.zeros((z.width_x, LANES), F32)
    for number, q in enumerate(UPWARD_MOVERS):
        here = (lane >= number * CZ) & (lane < (number + 1) * CZ)
        value = post_ref[q, :, z.plane - LANES :]
        up = jnp.where(here, pltpu.roll(value, (number + 1) * CZ, 1), up)
    for number, q in enumerate(DOWNWARD_MOVERS):
        here = (lane >= number * CZ) & (lane < (number + 1) * CZ)
        value = post_ref[q, :, :LANES]
        down = jnp.where(here, value if number == 0 else pltpu.roll(value, number * CZ, 1), down)
    up_ref[...] = up
    down_ref[...] = down


def stream(z, post_ref, from_left_ref, from_right_ref, below_ref, above_ref, out_ref, grid_ref, flow_ref):
    shape = (z.width_x, z.plane)
    lane = lane_index(shape)
    row = row_index(shape)
    edge_row = row_index((z.width_x, LANES))
    layer = lax.rem(lane, CZ)
    last_row = z.width_x - 1
    sums = [None] * 4
    for q in range(19):
        cx, cy, cz = LATTICE_VELOCITY[q]
        value = post_ref[q]
        if cx == 1:
            k = RIGHT_MOVERS.index(q)
            value = jnp.where(row == 0, from_left_ref[k : k + 1, :], pltpu.roll(value, 1, 0))
        elif cx == -1:
            k = LEFT_MOVERS.index(q)
            value = jnp.where(
                row == last_row, from_right_ref[k : k + 1, :], pltpu.roll(value, last_row, 0)
            )
        if cy:
            edges = below_ref if cy == 1 else above_ref
            k = (UPWARD_MOVERS if cy == 1 else DOWNWARD_MOVERS).index(q)
            edge = edges[: z.width_x, :]
            shift = (LANES - k * CZ if cy == 1 else 2 * LANES - (k + 1) * CZ) % LANES
            edge = edge if shift == 0 else pltpu.roll(edge, shift, 1)
            if cx:
                movers = RIGHT_MOVERS if cx == 1 else LEFT_MOVERS
                at = z.width_x + (0 if cx == 1 else 8) + movers.index(q)
                corner = edges[at : at + 1, :]
                turn = CZ if cy == 1 else LANES - CZ
                corner = pltpu.roll(corner, turn, 1)
                if cx == 1:
                    edge = jnp.where(edge_row == 0, corner, pltpu.roll(edge, 1, 0))
                else:
                    edge = jnp.where(edge_row == last_row, corner, pltpu.roll(edge, last_row, 0))
            rest = jnp.zeros((z.width_x, z.plane - LANES), F32)
            if cy == 1:
                wide = jnp.concatenate([edge, rest], axis=1)
                value = jnp.where(lane < CZ, wide, pltpu.roll(value, CZ, 1))
            else:
                wide = jnp.concatenate([rest, edge], axis=1)
                value = jnp.where(lane >= z.plane - CZ, wide, pltpu.roll(value, z.plane - CZ, 1))
        if cz == 1:
            value = jnp.where(
                layer == 0, pltpu.roll(value, z.plane - (CZ - 1), 1), pltpu.roll(value, 1, 1)
            )
        elif cz == -1:
            value = jnp.where(
                layer == CZ - 1, pltpu.roll(value, CZ - 1, 1), pltpu.roll(value, z.plane - 1, 1)
            )
        out_ref[q] = value
    for r in range(z.width_x // 8):
        rows = slice(r * 8, (r + 1) * 8)
        for t in range(z.plane // LANES):
            lanes = slice(t * LANES, (t + 1) * LANES)
            f = [out_ref[q, rows, lanes] for q in range(19)]
            density = f[0]
            for q in range(1, 19):
                density = density + f[q]
            inverse = 1.0 / density
            for c in range(3):
                m = (0.5 * PUSH_SCALE) * grid_ref[
                    c * z.width_x + r * 8 : c * z.width_x + (r + 1) * 8, lanes
                ]
                for q in range(1, 19):
                    v = LATTICE_VELOCITY[q][c]
                    if v == 1:
                        m = m + f[q]
                    elif v == -1:
                        m = m - f[q]
                sums[c] = m * inverse
            for c in range(3):
                flow_ref[c * z.width_x + r * 8 : c * z.width_x + (r + 1) * 8, lanes] = sums[c]


def first_kernel(z, *refs):
    d = z.devices_y
    messages = refs[:d]
    shape_ref, link_ref, degree_ref, flow_ref = refs[d : d + 4]
    grid_ref, post_ref, right_ref, left_ref, up_ref, down_ref = refs[d + 4 : d + 10]
    places_ref, stiff_ref, lists_ref = refs[d + 10 : d + 13]
    ends, force, plane, lift = refs[d + 13 :]
    for e in range(d):
        for h in range(3):
            split_message(z, messages[e][h], places_ref, ends, (3 * e + h) * CAP)
    place_tails(z, ends, places_ref, stiff_ref)
    list_slots(z, places_ref, stiff_ref, lists_ref)
    forces(z, places_ref, stiff_ref, shape_ref, link_ref, degree_ref, force)
    spread(z, places_ref, force, lists_ref, grid_ref, plane, lift)
    collide(z, flow_ref, grid_ref, post_ref)
    write_edges(z, post_ref, right_ref, left_ref, up_ref, down_ref)


def middle_kernel(z, *refs):
    post_ref, from_left, from_right, below, above = refs[:5]
    old_grid, old_places, stiff_ref, old_lists, shape_ref, link_ref, degree_ref = refs[5:12]
    grid_ref, next_ref, right_ref, left_ref, up_ref, down_ref, places_ref, lists_ref = refs[12:20]
    moved, flow, force, plane, lift = refs[20:]
    places_ref[...] = old_places[...]
    stream(z, post_ref, from_left, from_right, below, above, moved, old_grid, flow)
    sample(z, places_ref, flow, old_lists, plane)
    list_slots(z, places_ref, stiff_ref, lists_ref)
    forces(z, places_ref, stiff_ref, shape_ref, link_ref, degree_ref, force)
    spread(z, places_ref, force, lists_ref, grid_ref, plane, lift)
    collide(z, moved, grid_ref, next_ref)
    write_edges(z, next_ref, right_ref, left_ref, up_ref, down_ref)


def join_message(z, places_ref, slot, out_ref, at):
    lane = lane_index((CAP, LANES))
    ends = jnp.zeros((CAP, LANES), F32)
    for c in range(3):
        line = places_ref[c, slot : slot + CAP, :]
        out_ref[at, :, c * z.main : (c + 1) * z.main] = line[:, : z.main]
        end = jnp.where(lane < z.tail, line[:, z.main :], 0.0)
        ends = ends + (end if c == 0 else pltpu.roll(end, c * z.tail, 1))
    out_ref[at, :, 3 * z.main :] = ends


def last_kernel(z, *refs):
    d = z.devices_y
    post_ref, from_left, from_right, below, above, grid_ref, old_places, lists_ref = refs[:8]
    moved_ref = refs[8]
    message_refs = refs[9 : 9 + d]
    flow, places, plane = refs[9 + d :]
    places[...] = old_places[...]
    stream(z, post_ref, from_left, from_right, below, above, moved_ref, grid_ref, flow)
    sample(z, places, flow, lists_ref, plane)
    for e in range(d):
        for h in range(3):
            join_message(z, places, (3 * e + h) * CAP, message_refs[e], h)


def shift(value, axis, step):
    count = lax.axis_size(axis)
    return lax.ppermute(value, axis, [(i, (i + step) % count) for i in range(count)])


def trade_edges(z, right, left, up, down):
    from_left = shift(right, "gx", 1)
    from_right = shift(left, "gx", -1)
    far, near = slice(z.plane - LANES, z.plane), slice(0, LANES)
    up = jnp.concatenate([up, from_left[:, far], from_right[:, far]], axis=0)
    down = jnp.concatenate([down, from_left[:, near], from_right[:, near]], axis=0)
    return from_left, from_right, shift(up, "gy", 1), shift(down, "gy", -1)


def local(populations, positions, stiffness, membrane_shape, neighbours, home_tile):
    z = Sizes(
        positions.shape[0],
        positions.shape[2],
        populations.shape[1],
        populations.shape[2],
        lax.axis_size("gx"),
        lax.axis_size("gy"),
    )
    d = z.devices_y
    run = functools.partial
    line = (CAP, z.message)
    table = VMEM((z.groups,) + line, F32)
    counts = SMEM((z.groups,), jnp.int32)
    places_in = positions.transpose(1, 0, 2)
    to_left, center, to_right = call(
        run(pack_kernel, z),
        [((d,) + line, F32, VMEM)] * 3,
        [SMEM, SMEM, VMEM],
        [table, counts],
    )(home_tile, stiffness, places_in)
    from_left = shift(to_right, "gx", 1)
    from_right = shift(to_left, "gx", -1)
    messages = [jnp.stack([center[e], from_left[e], from_right[e]]) for e in range(d)]
    messages = [messages[0]] + [shift(messages[e], "gy", e) for e in range(1, d)]
    link, degree, shape = call(
        run(matrix_kernel, z),
        [
            ((z.full, z.full), BF16, VMEM),
            ((1, z.full), F32, VMEM),
            ((3, z.full), F32, VMEM),
        ],
        [VMEM, VMEM],
        [VMEM((z.full, z.full), F32)],
        pl.CostEstimate(flops=2_000_000_000, bytes_accessed=4_000_000, transcendentals=0),
    )(neighbours.T, membrane_shape)

    grid_type = ((3 * z.width_x, z.plane), F32, VMEM)
    post_type = ((19, z.width_x, z.plane), F32, VMEM)
    plane_scratch = VMEM((z.plane, 2 * z.main), BF16)
    lift_scratch = VMEM((3 * z.width_x, 2 * z.main), BF16)
    edge_types = [((8, z.plane), F32, VMEM)] * 2 + [((z.width_x, LANES), F32, VMEM)] * 2
    places_type = ((3, z.slots, z.full), F32, VMEM)
    lists_type = ((LISTS,), jnp.int32, SMEM)
    rows = VMEM(places_type[0], F32)

    grid, post, right, left, up, down, places, stiff, lists = call(
        run(first_kernel, z),
        [grid_type, post_type]
        + edge_types
        + [places_type, ((z.slots, LANES), F32, VMEM), lists_type],
        [VMEM] * (d + 4),
        [VMEM((z.slots, LANES), F32), rows, plane_scratch, lift_scratch],
    )(*messages, shape, link, degree, populations)
    for _ in range(STEPS - 1):
        edges = trade_edges(z, right, left, up, down)
        grid, post, right, left, up, down, places, lists = call(
            run(middle_kernel, z),
            [grid_type, post_type] + edge_types + [places_type, lists_type],
            [VMEM] * 8 + [SMEM] + [VMEM] * 3,
            [VMEM(post_type[0], F32), VMEM(grid_type[0], F32), rows, plane_scratch, lift_scratch],
        )(post, *edges, grid, places, stiff, lists, shape, link, degree)
    edges = trade_edges(z, right, left, up, down)
    moved, *messages = call(
        run(last_kernel, z),
        [post_type] + [((3,) + line, F32, VMEM)] * d,
        [VMEM] * 7 + [SMEM],
        [VMEM(grid_type[0], F32), rows, plane_scratch],
    )(post, *edges, grid, places, lists)
    messages = [messages[0]] + [shift(messages[e], "gy", -e) for e in range(1, d)]
    right_part = shift(jnp.stack([m[1] for m in messages]), "gx", -1)
    left_part = shift(jnp.stack([m[2] for m in messages]), "gx", 1)
    (displacement,) = call(
        run(unpack_kernel, z),
        [(places_in.shape, F32, VMEM)],
        [SMEM] + [VMEM] * (3 + d),
        [table, counts],
    )(home_tile, places_in, left_part, right_part, *messages)
    return moved, displacement.transpose(1, 0, 2), grid.reshape(3, z.width_x, z.plane)


def solution(mesh):
    placed = (
        P(None, "gx", "gy"),
        P(("gx", "gy"), None, None),
        P(("gx", "gy")),
        P(),
        P(),
        P(("gx", "gy")),
    )
    return jax.shard_map(
        local,
        mesh=mesh,
        in_specs=placed,
        out_specs=(P(None, "gx", "gy"), P(("gx", "gy"), None, None), P(None, "gx", "gy")),
        check_vma=False,
    )
```

```python
import functools

import jax
import jax.numpy as jnp
from jax import lax
from jax.experimental import pallas as pl
from jax.experimental.pallas import tpu as pltpu
from jax.sharding import PartitionSpec as P

CZ = 16
CAP = 4
STEPS = 2

LATTICE_VELOCITY = [
    [0, 0, 0],
    [1, 0, 0],
    [-1, 0, 0],
    [0, 1, 0],
    [0, -1, 0],
    [0, 0, 1],
    [0, 0, -1],
    [1, 1, 0],
    [-1, -1, 0],
    [1, -1, 0],
    [-1, 1, 0],
    [1, 0, 1],
    [-1, 0, -1],
    [1, 0, -1],
    [-1, 0, 1],
    [0, 1, 1],
    [0, -1, -1],
    [0, 1, -1],
    [0, -1, 1],
]
LATTICE_WEIGHT = [1.0 / 3.0] + [1.0 / 18.0] * 6 + [1.0 / 36.0] * 12
RIGHT_MOVERS = [1, 7, 9, 11, 13]
LEFT_MOVERS = [2, 8, 10, 12, 14]
UPWARD_MOVERS = [3, 7, 10, 15, 17]
DOWNWARD_MOVERS = [4, 8, 9, 16, 18]
RELAX_RATE = 1.25
PUSH_SCALE = 0.05
TETHER_GAIN = 2.0
LANES = 128
WINDOW = 16
SLOW = 15
FAST_AT = 2
SLOW_AT = 64
CODE_AT = 128
LISTS = 192
F32 = jnp.float32
BF16 = jnp.bfloat16
SMEM = pltpu.SMEM
VMEM = pltpu.VMEM
HBM = pltpu.MemorySpace.HBM


def spec(space):
    return pl.BlockSpec(memory_space=space)


def call(kernel, outs, ins, scratch=(), cost=None, limit=None):
    return pl.pallas_call(
        kernel,
        out_shape=[jax.ShapeDtypeStruct(s, d) for s, d, _ in outs],
        in_specs=[spec(m) for m in ins],
        out_specs=[spec(m) for _, _, m in outs],
        scratch_shapes=list(scratch),
        compiler_params=pltpu.CompilerParams(vmem_limit_bytes=limit or (24 << 20)),
        cost_estimate=cost,
    )


def lane_index(shape):
    return lax.broadcasted_iota(jnp.int32, shape, len(shape) - 1)


def row_index(shape):
    return lax.broadcasted_iota(jnp.int32, shape, len(shape) - 2)


class Sizes:
    def __init__(self, cells, vertices, width_x, plane, devices_x, devices_y):
        self.cells = cells
        self.vertices = vertices
        self.width_x = width_x
        self.plane = plane
        self.devices_x = devices_x
        self.devices_y = devices_y
        self.main = vertices - vertices % LANES
        self.tail = vertices - self.main
        self.full = self.main + LANES
        self.message = 3 * self.main + LANES
        self.groups = 3 * devices_y
        self.slots = 3 * devices_y * CAP
        self.rows = self.slots + 8
        self.width_y = plane // CZ


def cell_places(z, home_ref, count_ref):
    own_x = lax.axis_index("gx")
    own_y = lax.axis_index("gy")
    for g in range(z.groups):
        count_ref[g] = 0
    found = []
    for n in range(z.cells):
        home = home_ref[n]
        target_x = lax.div(home, z.devices_y)
        target_y = lax.rem(home, z.devices_y)
        side = lax.rem(target_x - own_x + 1 + z.devices_x, z.devices_x)
        turn = lax.bitwise_xor(target_y, own_y)
        group = side * z.devices_y + turn
        rank = count_ref[group]
        count_ref[group] = rank + 1
        found.append((group, rank))
    return found


def pack_kernel(z, home_in, stiff_in, places_in, left_ref, center_ref, right_ref, *scratch):
    home_ref, stiff_ref, places_ref, table_ref, count_ref, sem = scratch
    copies = [
        pltpu.make_async_copy(source, target, sem.at[k])
        for k, (source, target) in enumerate(
            [(home_in, home_ref), (stiff_in, stiff_ref), (places_in, places_ref)]
        )
    ]
    for copy in copies:
        copy.start()
    table_ref[...] = jnp.zeros_like(table_ref)
    for copy in copies:
        copy.wait()
    lane = lane_index((1, LANES))
    zeros = jnp.zeros((1, LANES - z.tail), F32)
    for n, (group, rank) in enumerate(cell_places(z, home_ref, count_ref)):
        ends = jnp.where(lane == 3 * z.tail, stiff_ref[n], 0.0)
        parts = []
        for c in range(3):
            line = places_ref[c, n : n + 1, :]
            parts.append(line[:, : z.main])
            end = jnp.concatenate([line[:, z.main :], zeros], axis=1)
            ends = ends + (end if c == 0 else pltpu.roll(end, c * z.tail, 1))
        table_ref[group, pl.ds(rank, 1), :] = jnp.concatenate(parts + [ends], axis=1)
    d = z.devices_y
    left_ref[...] = table_ref[0:d]
    center_ref[...] = table_ref[d : 2 * d]
    right_ref[...] = table_ref[2 * d : 3 * d]


def unpack_kernel(z, home_ref, places_ref, left_ref, right_ref, *rest):
    center_refs = rest[: z.devices_y]
    out_ref, table_ref, count_ref = rest[z.devices_y :]
    d = z.devices_y
    table_ref[0:d] = left_ref[...]
    table_ref[2 * d : 3 * d] = right_ref[...]
    for r in range(d):
        table_ref[d + r] = center_refs[r][0]
    for n, (group, rank) in enumerate(cell_places(z, home_ref, count_ref)):
        line = table_ref[group, pl.ds(rank, 1), :]
        ends = line[:, 3 * z.main :]
        for c in range(3):
            end = ends if c == 0 else pltpu.roll(ends, LANES - c * z.tail, 1)
            whole = jnp.concatenate([line[:, c * z.main : (c + 1) * z.main], end], axis=1)
            out_ref[c, n : n + 1, :] = whole[:, : z.vertices] - places_ref[c, n : n + 1, :]


def matrix_kernel(z, near_in, shape_in, after_in, link_ref, degree_ref, rest_ref, *scratch):
    near_ref, shape_ref, half_ref, sem = scratch
    copies = [
        pltpu.make_async_copy(near_in, near_ref, sem.at[0]),
        pltpu.make_async_copy(shape_in, shape_ref, sem.at[1]),
    ]
    for copy in copies:
        copy.start()
    for copy in copies:
        copy.wait()
    near = near_ref[...]
    shape = shape_ref[...]
    rest_ref[...] = jnp.concatenate(
        [shape, jnp.zeros((3, z.full - z.vertices), F32)], axis=1
    )
    entries = near.shape[0]
    tiles = z.full // LANES
    missing = jnp.full((entries, z.full - z.vertices), -1, jnp.int32)
    near = jnp.concatenate([near, missing], axis=1)
    row = row_index((LANES, LANES))
    for t in range(tiles):
        lines = near[:, t * LANES : (t + 1) * LANES]
        for r in range(tiles):
            total = jnp.zeros((LANES, LANES), F32)
            for b in range(entries):
                total += jnp.where(lines[b : b + 1] == row + r * LANES, 1.0, 0.0)
            half_ref[r * LANES : (r + 1) * LANES, t * LANES : (t + 1) * LANES] = total
    for t in range(tiles):
        lanes = slice(t * LANES, (t + 1) * LANES)
        degree = jnp.zeros((1, LANES), F32) + TETHER_GAIN
        for r in range(tiles):
            rows = slice(r * LANES, (r + 1) * LANES)
            total = half_ref[rows, lanes] + half_ref[lanes, rows].T
            link_ref[rows, lanes] = total.astype(BF16)
            degree += jnp.sum(total, axis=0, keepdims=True)
        degree_ref[:, lanes] = degree


def split_message(z, value, places_ref, ends_ref, slot):
    for c in range(3):
        places_ref[c, slot : slot + CAP, : z.main] = value[:, c * z.main : (c + 1) * z.main]
    ends_ref[slot : slot + CAP, :] = value[:, 3 * z.main :]


def place_tails(z, ends_ref, places_ref, stiff_ref):
    ends = ends_ref[...]
    lane = lane_index(ends.shape)
    for c in range(3):
        end = ends if c == 0 else pltpu.roll(ends, LANES - c * z.tail, 1)
        places_ref[c, : z.slots, z.main :] = jnp.where(lane < z.tail, end, 0.0)
        places_ref[c, z.slots :, :] = jnp.zeros((8, z.full), F32)
    stiff_ref[...] = jnp.broadcast_to(ends[:, 3 * z.tail : 3 * z.tail + 1], ends.shape)


def forces(z, places_ref, stiff_ref, shape_ref, link_ref, degree_ref, force_ref):
    rows = z.slots
    lane = lane_index((rows, z.full))
    inside = lane < z.vertices
    parts = []
    for c in range(3):
        x = places_ref[c, :rows, :]
        mean = jnp.sum(x, axis=1, keepdims=True) * (1.0 / z.vertices)
        parts.append(jnp.where(inside, x - mean - shape_ref[c : c + 1, :], 0.0))
    strain = jnp.concatenate(parts, axis=0)
    high = strain.astype(BF16)
    rest = strain - high.astype(F32)
    low = rest.astype(BF16)
    both = jnp.dot(
        jnp.concatenate([high, low], axis=0), link_ref[...], preferred_element_type=F32
    )
    linked = both[: 3 * rows] + both[3 * rows :]
    pulled = degree_ref[...] * (high.astype(F32) + low.astype(F32)) - linked
    stiff = stiff_ref[:, 0:1]
    for c in range(3):
        force_ref[c, :rows, :] = -stiff * pulled[c * rows : (c + 1) * rows]
        force_ref[c, rows:, :] = jnp.zeros((8, z.full), F32)


def list_slots(z, places_ref, stiff_ref, lists_ref):
    codes = None
    fits = None
    for c, width in ((0, z.width_x), (1, z.width_y)):
        x = places_ref[c, : z.slots, : z.main]
        low = jnp.maximum(jnp.floor(jnp.min(x, axis=1, keepdims=True)), 0.0)
        high = jnp.minimum(jnp.floor(jnp.max(x, axis=1, keepdims=True)) + 1.0, width - 1.0)
        block = jnp.minimum(jnp.floor(low * 0.125), (width - WINDOW) // 8 * 1.0)
        fit = high - 8.0 * block <= WINDOW - 1.0
        codes = block if codes is None else codes + 4.0 * block
        fits = fit if fits is None else fits & fit
    codes = jnp.where(fits, codes, SLOW * 1.0)
    codes = jnp.where(stiff_ref[:, 0:1] > 0.0, codes, -1.0).astype(jnp.int32)
    fast, slow = jnp.int32(0), jnp.int32(0)
    for s in range(z.slots):
        code = codes[s, 0]
        lists_ref[CODE_AT + s] = code
        lists_ref[FAST_AT + fast] = s
        lists_ref[SLOW_AT + slow] = s
        fast = fast + jnp.where((code >= 0) & (code < SLOW), 1, 0)
        slow = slow + jnp.where(code == SLOW, 1, 0)
    lists_ref[CODE_AT + z.slots] = 0
    for k in range(6):
        lists_ref[FAST_AT + fast + k] = z.slots
    lists_ref[0] = lax.div(fast + 3, 4)
    lists_ref[1] = slow


def window_of(lists_ref, s):
    code = lists_ref[CODE_AT + s]
    return 8 * lax.rem(code, 4), 8 * lax.div(code, 4)


def tails_to_lanes(z, ref, c):
    ends = ref[c, : z.slots, z.main :]
    lane = lane_index(ends.shape)
    row = row_index(ends.shape)
    picked = jnp.zeros_like(ends)
    for t in range(z.tail):
        picked = jnp.where(lane == row * z.tail + t, ends[:, t : t + 1], picked)
    return jnp.sum(picked, axis=0, keepdims=True)


def hat(gap):
    return jnp.maximum(0.0, 1.0 - gap)


def hat_depth(depth):
    steps = row_index((CZ, depth.shape[1])).astype(F32)
    wrapped = depth - CZ * jnp.floor(depth * (1.0 / CZ))
    gap = jnp.abs(wrapped - steps)
    return hat(jnp.minimum(gap, CZ - gap))


def whole_tables(z, line, plane_ref):
    x, y, depth = line
    width = x.shape[1]
    hat_x = hat(jnp.abs(x - row_index((z.width_x, width)).astype(F32)))
    hat_y = hat(jnp.abs(y - row_index((z.width_y, width)).astype(F32)))
    hat_z = hat_depth(depth)
    for j in range(z.width_y):
        plane_ref[j * CZ : (j + 1) * CZ, :width] = (hat_y[j : j + 1] * hat_z).astype(BF16)
    return hat_x


def window_tables(line, first, plane_ref, rows_at, rows_ref):
    x, y, depth = line
    steps = row_index((WINDOW, x.shape[1])).astype(F32)
    hat_x = hat(jnp.abs(x - (steps + first[0].astype(F32))))
    rows_ref[...] = hat(jnp.abs(y - (steps + first[1].astype(F32))))
    hat_z = hat_depth(depth)
    for j in range(WINDOW):
        hat_y = rows_ref[pl.ds(j, 8, stride=0), :]
        block = jnp.concatenate(
            [hat_y * hat_z[k * 8 : (k + 1) * 8] for k in range(CZ // 8)], axis=0
        )
        plane_ref[rows_at + j * CZ : rows_at + (j + 1) * CZ, :] = block.astype(BF16)
    return hat_x


def contract(lift, plane):
    return lax.dot_general(lift, plane, (((1,), (1,)), ((), ())), preferred_element_type=F32)


PLANE_ROWS = WINDOW * CZ
LIFT_ROWS = 3 * WINDOW


def fast_pairs(lists_ref, build, use):
    def entry(pair, h):
        s = lists_ref[FAST_AT + 2 * pair + h]
        return s, window_of(lists_ref, s)

    def pair(p):
        return [entry(p, h) for h in range(2)]

    def step(q, carry):
        build(pair(2 * q + 1), 1)
        use(pair(2 * q), 0)
        build(pair(2 * q + 2), 0)
        use(pair(2 * q + 1), 1)
        return carry

    build(pair(0), 0)
    lax.fori_loop(0, lists_ref[0], step, 0)


def spread(z, places_ref, force_ref, lists_ref, grid_ref, buffers):
    planes, lifts, hats, _ = buffers

    def lift_up(pull, hat_x, lift_ref, row):
        count, width = hat_x.shape
        for c in range(3):
            rows = slice(row + c * count, row + (c + 1) * count)
            lift_ref[rows, :width] = (pull[c] * hat_x).astype(BF16)

    def load(s):
        line = [places_ref[c, pl.ds(s, 1), : z.main] for c in range(3)]
        pull = [force_ref[c, pl.ds(s, 1), : z.main] for c in range(3)]
        return line, pull

    def build(pair, b):
        for h, (s, first) in enumerate(pair):
            line, pull = load(s)
            hat_x = window_tables(line, first, planes[b], h * PLANE_ROWS, hats[2 * b + h])
            lift_up(pull, hat_x, lifts[b], h * LIFT_ROWS)

    def use(pair, b):
        for h, (_, first) in enumerate(pair):
            part = contract(
                lifts[b][h * LIFT_ROWS : (h + 1) * LIFT_ROWS, :],
                planes[b][h * PLANE_ROWS : (h + 1) * PLANE_ROWS, :],
            )
            lanes = pl.ds(pl.multiple_of(first[1] * CZ, LANES), PLANE_ROWS)
            for c in range(3):
                rows = pl.ds(pl.multiple_of(c * z.width_x + first[0], 8), WINDOW)
                grid_ref[rows, lanes] += part[c * WINDOW : (c + 1) * WINDOW]

    def slow(p, carry):
        line, pull = load(lists_ref[SLOW_AT + p])
        lift_up(pull, whole_tables(z, line, planes[0]), lifts[0], 0)
        grid_ref[...] += contract(lifts[0][...], planes[0][...])
        return carry

    line = [tails_to_lanes(z, places_ref, c) for c in range(3)]
    pull = [tails_to_lanes(z, force_ref, c) for c in range(3)]
    lift_up(pull, whole_tables(z, line, planes[1]), lifts[1], 0)
    grid_ref[...] = contract(lifts[1][:, :LANES], planes[1][:, :LANES])
    fast_pairs(lists_ref, build, use)
    lax.fori_loop(0, lists_ref[1], slow, 0)


def sample(z, places_ref, flow_ref, lists_ref, buffers):
    planes, _, hats, hats_x = buffers

    def load(s):
        return [places_ref[c, pl.ds(s, 1), : z.main] for c in range(3)]

    def move(s, picked, hat_x):
        count = hat_x.shape[0]
        for c in range(3):
            drift = jnp.sum(picked[c * count : (c + 1) * count] * hat_x, axis=0, keepdims=True)
            places_ref[c, pl.ds(s, 1), : z.main] = places_ref[c, pl.ds(s, 1), : z.main] + drift

    def build(pair, b):
        for h, (s, first) in enumerate(pair):
            hats_x[2 * b + h][...] = window_tables(
                load(s), first, planes[b], h * PLANE_ROWS, hats[2 * b + h]
            )

    def use(pair, b):
        picked = []
        for h, (_, first) in enumerate(pair):
            lanes = pl.ds(pl.multiple_of(first[1] * CZ, LANES), PLANE_ROWS)
            flow = [
                flow_ref[pl.ds(pl.multiple_of(c * z.width_x + first[0], 8), WINDOW), lanes]
                for c in range(3)
            ]
            picked.append(
                jnp.dot(
                    jnp.concatenate(flow, axis=0).astype(BF16),
                    planes[b][h * PLANE_ROWS : (h + 1) * PLANE_ROWS, :],
                    preferred_element_type=F32,
                )
            )
        for h, (s, _) in enumerate(pair):
            move(s, picked[h], hats_x[2 * b + h][...])

    def slow(p, carry):
        s = lists_ref[SLOW_AT + p]
        hat_x = whole_tables(z, load(s), planes[0])
        picked = jnp.dot(flow_ref[...].astype(BF16), planes[0][...], preferred_element_type=F32)
        move(s, picked, hat_x)
        return carry

    line = [tails_to_lanes(z, places_ref, c) for c in range(3)]
    hat_x = whole_tables(z, line, planes[1])
    picked = jnp.dot(
        flow_ref[...].astype(BF16), planes[1][:, :LANES], preferred_element_type=F32
    )
    rows = z.slots
    lane = lane_index((rows, LANES))
    row = row_index((rows, LANES))
    for c in range(3):
        drift = jnp.sum(picked[c * z.width_x : (c + 1) * z.width_x] * hat_x, axis=0, keepdims=True)
        ends = places_ref[c, :rows, z.main :]
        for t in range(z.tail):
            moved = jnp.sum(
                jnp.where(lane == row * z.tail + t, drift, 0.0), axis=1, keepdims=True
            )
            ends = jnp.where(lane == t, ends + moved, ends)
        places_ref[c, :rows, z.main :] = ends
    fast_pairs(lists_ref, build, use)
    lax.fori_loop(0, lists_ref[1], slow, 0)


def collide(z, flow_ref, grid_ref, post_ref):
    def block(r, carry):
        rows = pl.ds(pl.multiple_of(r * 8, 8), 8)
        for t in range(z.plane // LANES):
            lanes = slice(t * LANES, (t + 1) * LANES)
            f = [flow_ref[q, rows, lanes] for q in range(19)]
            push = [
                PUSH_SCALE
                * grid_ref[pl.ds(pl.multiple_of(c * z.width_x + r * 8, 8), 8), lanes]
                for c in range(3)
            ]
            density = f[0]
            for q in range(1, 19):
                density = density + f[q]
            inverse = 1.0 / density
            u = []
            for c in range(3):
                m = 0.5 * push[c]
                for q in range(1, 19):
                    v = LATTICE_VELOCITY[q][c]
                    if v == 1:
                        m = m + f[q]
                    elif v == -1:
                        m = m - f[q]
                u.append(m * inverse)
            square = u[0] * u[0] + u[1] * u[1] + u[2] * u[2]
            work = u[0] * push[0] + u[1] * push[1] + u[2] * push[2]
            gain = 1.0 - 0.5 * RELAX_RATE
            heavy = RELAX_RATE * density
            base = heavy * (1.0 - 1.5 * square) - (3.0 * gain) * work
            post_ref[0, rows, lanes] = (1.0 - RELAX_RATE) * f[0] + LATTICE_WEIGHT[0] * base
            for q in range(1, 19, 2):
                along = None
                pull = None
                for c in range(3):
                    v = LATTICE_VELOCITY[q][c]
                    if v:
                        along = v * u[c] if along is None else along + v * u[c]
                        pull = v * push[c] if pull is None else pull + v * push[c]
                w = LATTICE_WEIGHT[q]
                lifted = heavy * along
                even = w * (base + along * (4.5 * lifted + (9.0 * gain) * pull))
                odd = (3.0 * w) * (lifted + gain * pull)
                post_ref[q, rows, lanes] = (1.0 - RELAX_RATE) * f[q] + (even + odd)
                post_ref[q + 1, rows, lanes] = (1.0 - RELAX_RATE) * f[q + 1] + (even - odd)
        return carry

    lax.fori_loop(0, z.width_x // 8, block, 0)


def write_edges(z, post_ref, right_ref, left_ref, up_ref, down_ref):
    for number, q in enumerate(RIGHT_MOVERS):
        right_ref[number : number + 1, :] = post_ref[q, z.width_x - 1 : z.width_x, :]
    for number, q in enumerate(LEFT_MOVERS):
        left_ref[number : number + 1, :] = post_ref[q, 0:1, :]
    right_ref[5:8, :] = jnp.zeros((3, z.plane), F32)
    left_ref[5:8, :] = jnp.zeros((3, z.plane), F32)
    lane = lane_index((z.width_x, LANES))
    up = jnp.zeros((z.width_x, LANES), F32)
    down = jnp.zeros((z.width_x, LANES), F32)
    for number, q in enumerate(UPWARD_MOVERS):
        here = (lane >= number * CZ) & (lane < (number + 1) * CZ)
        value = post_ref[q, :, z.plane - LANES :]
        up = jnp.where(here, pltpu.roll(value, (number + 1) * CZ, 1), up)
    for number, q in enumerate(DOWNWARD_MOVERS):
        here = (lane >= number * CZ) & (lane < (number + 1) * CZ)
        value = post_ref[q, :, :LANES]
        down = jnp.where(here, value if number == 0 else pltpu.roll(value, number * CZ, 1), down)
    up_ref[...] = up
    down_ref[...] = down


def stream(z, post_ref, from_left_ref, from_right_ref, below_ref, above_ref, out_ref, grid_ref, flow_ref):
    shape = (z.width_x, z.plane)
    lane = lane_index(shape)
    row = row_index(shape)
    edge_row = row_index((z.width_x, LANES))
    layer = lax.rem(lane, CZ)
    last_row = z.width_x - 1
    sums = [None] * 4
    for q in range(19):
        cx, cy, cz = LATTICE_VELOCITY[q]
        value = post_ref[q]
        if cx == 1:
            k = RIGHT_MOVERS.index(q)
            value = jnp.where(row == 0, from_left_ref[k : k + 1, :], pltpu.roll(value, 1, 0))
        elif cx == -1:
            k = LEFT_MOVERS.index(q)
            value = jnp.where(
                row == last_row, from_right_ref[k : k + 1, :], pltpu.roll(value, last_row, 0)
            )
        if cy:
            edges = below_ref if cy == 1 else above_ref
            k = (UPWARD_MOVERS if cy == 1 else DOWNWARD_MOVERS).index(q)
            edge = edges[: z.width_x, :]
            shift = (LANES - k * CZ if cy == 1 else 2 * LANES - (k + 1) * CZ) % LANES
            edge = edge if shift == 0 else pltpu.roll(edge, shift, 1)
            if cx:
                movers = RIGHT_MOVERS if cx == 1 else LEFT_MOVERS
                at = z.width_x + (0 if cx == 1 else 8) + movers.index(q)
                corner = edges[at : at + 1, :]
                turn = CZ if cy == 1 else LANES - CZ
                corner = pltpu.roll(corner, turn, 1)
                if cx == 1:
                    edge = jnp.where(edge_row == 0, corner, pltpu.roll(edge, 1, 0))
                else:
                    edge = jnp.where(edge_row == last_row, corner, pltpu.roll(edge, last_row, 0))
            rest = jnp.zeros((z.width_x, z.plane - LANES), F32)
            if cy == 1:
                wide = jnp.concatenate([edge, rest], axis=1)
                value = jnp.where(lane < CZ, wide, pltpu.roll(value, CZ, 1))
            else:
                wide = jnp.concatenate([rest, edge], axis=1)
                value = jnp.where(lane >= z.plane - CZ, wide, pltpu.roll(value, z.plane - CZ, 1))
        if cz == 1:
            value = jnp.where(
                layer == 0, pltpu.roll(value, z.plane - (CZ - 1), 1), pltpu.roll(value, 1, 1)
            )
        elif cz == -1:
            value = jnp.where(
                layer == CZ - 1, pltpu.roll(value, CZ - 1, 1), pltpu.roll(value, z.plane - 1, 1)
            )
        out_ref[q] = value
    for r in range(z.width_x // 8):
        rows = slice(r * 8, (r + 1) * 8)
        for t in range(z.plane // LANES):
            lanes = slice(t * LANES, (t + 1) * LANES)
            f = [out_ref[q, rows, lanes] for q in range(19)]
            density = f[0]
            for q in range(1, 19):
                density = density + f[q]
            inverse = 1.0 / density
            for c in range(3):
                m = (0.5 * PUSH_SCALE) * grid_ref[
                    c * z.width_x + r * 8 : c * z.width_x + (r + 1) * 8, lanes
                ]
                for q in range(1, 19):
                    v = LATTICE_VELOCITY[q][c]
                    if v == 1:
                        m = m + f[q]
                    elif v == -1:
                        m = m - f[q]
                sums[c] = m * inverse
            for c in range(3):
                flow_ref[c * z.width_x + r * 8 : c * z.width_x + (r + 1) * 8, lanes] = sums[c]


def buffer_types(z):
    plane = VMEM((z.plane, z.main), BF16)
    lift = VMEM((3 * z.width_x, z.main), BF16)
    rows = VMEM((WINDOW, z.main), F32)
    return [plane] * 2 + [lift] * 2 + [rows] * 8


def split_buffers(refs):
    return refs[:2], refs[2:4], refs[4:8], refs[8:12]


def first_kernel(z, *refs):
    d = z.devices_y
    messages = refs[:d]
    shape_ref, link_ref, degree_ref, flow_ref = refs[d : d + 4]
    grid_ref, post_ref, right_ref, left_ref, up_ref, down_ref = refs[d + 4 : d + 10]
    places_ref, stiff_ref = refs[d + 10 : d + 12]
    ends, force, lists = refs[d + 12 : d + 15]
    buffers = split_buffers(refs[d + 15 :])
    for e in range(d):
        for h in range(3):
            split_message(z, messages[e][h], places_ref, ends, (3 * e + h) * CAP)
    place_tails(z, ends, places_ref, stiff_ref)
    list_slots(z, places_ref, stiff_ref, lists)
    forces(z, places_ref, stiff_ref, shape_ref, link_ref, degree_ref, force)
    spread(z, places_ref, force, lists, grid_ref, buffers)
    collide(z, flow_ref, grid_ref, post_ref)
    write_edges(z, post_ref, right_ref, left_ref, up_ref, down_ref)


def sort_edges(near_ref, far_ref, below_ref, above_ref):
    even = lax.rem(lax.axis_index("gy"), 2) == 0

    @pl.when(even)
    def _():
        above_ref[...] = near_ref[...]
        below_ref[...] = far_ref[...]

    @pl.when(jnp.logical_not(even))
    def _():
        below_ref[...] = near_ref[...]
        above_ref[...] = far_ref[...]


def middle_kernel(z, *refs):
    post_ref, from_left, from_right, near, far = refs[:5]
    old_grid, old_places, stiff_ref, shape_ref, link_ref, degree_ref = refs[5:11]
    grid_ref, next_ref, right_ref, left_ref, up_ref, down_ref, places_ref = refs[11:18]
    moved, flow, below, above, force, lists = refs[18:24]
    buffers = split_buffers(refs[24:])
    sort_edges(near, far, below, above)
    places_ref[...] = old_places[...]
    list_slots(z, places_ref, stiff_ref, lists)
    stream(z, post_ref, from_left, from_right, below, above, moved, old_grid, flow)
    sample(z, places_ref, flow, lists, buffers)
    list_slots(z, places_ref, stiff_ref, lists)
    forces(z, places_ref, stiff_ref, shape_ref, link_ref, degree_ref, force)
    spread(z, places_ref, force, lists, grid_ref, buffers)
    collide(z, moved, grid_ref, next_ref)
    write_edges(z, next_ref, right_ref, left_ref, up_ref, down_ref)


def join_message(z, places_ref, slot, out_ref, at):
    lane = lane_index((CAP, LANES))
    ends = jnp.zeros((CAP, LANES), F32)
    for c in range(3):
        line = places_ref[c, slot : slot + CAP, :]
        out_ref[at, :, c * z.main : (c + 1) * z.main] = line[:, : z.main]
        end = jnp.where(lane < z.tail, line[:, z.main :], 0.0)
        ends = ends + (end if c == 0 else pltpu.roll(end, c * z.tail, 1))
    out_ref[at, :, 3 * z.main :] = ends


def last_kernel(z, *refs):
    d = z.devices_y
    post_ref, from_left, from_right, near, far, grid_ref, old_places, stiff_ref = refs[:8]
    moved_ref, density_ref = refs[8:10]
    message_refs = refs[10 : 10 + d]
    flow, below, above, places, lists = refs[10 + d : 15 + d]
    buffers = split_buffers(refs[15 + d :])
    sort_edges(near, far, below, above)
    density_ref[...] = grid_ref[...]
    places[...] = old_places[...]
    list_slots(z, places, stiff_ref, lists)
    stream(z, post_ref, from_left, from_right, below, above, moved_ref, grid_ref, flow)
    sample(z, places, flow, lists, buffers)
    for e in range(d):
        for h in range(3):
            join_message(z, places, (3 * e + h) * CAP, message_refs[e], h)


def shift(value, axis, step):
    count = lax.axis_size(axis)
    return lax.ppermute(value, axis, [(i, (i + step) % count) for i in range(count)])


def swap(value, axis, key):
    count = lax.axis_size(axis)
    return lax.ppermute(value, axis, [(i, i ^ key) for i in range(count)])


def swap_across(value, axis):
    count = lax.axis_size(axis)
    return lax.ppermute(
        value, axis, [(i, (i + 1) % count if i % 2 else (i - 1) % count) for i in range(count)]
    )


def trade_edges(z, right, left, up, down):
    from_left = shift(right, "gx", 1)
    from_right = shift(left, "gx", -1)
    far, near = slice(z.plane - LANES, z.plane), slice(0, LANES)
    up = jnp.concatenate([up, from_left[:, far], from_right[:, far]], axis=0)
    down = jnp.concatenate([down, from_left[:, near], from_right[:, near]], axis=0)
    even = lax.rem(lax.axis_index("gy"), 2) == 0
    across = swap_across(jnp.where(even, down, up), "gy")
    beside = swap(jnp.where(even, up, down), "gy", 1)
    return from_left, from_right, beside, across


def local(populations, positions, stiffness, membrane_shape, neighbours, home_tile):
    z = Sizes(
        positions.shape[0],
        positions.shape[2],
        populations.shape[1],
        populations.shape[2],
        lax.axis_size("gx"),
        lax.axis_size("gy"),
    )
    d = z.devices_y
    turns = range(d - 1, 0, -1)
    run = functools.partial
    line = (CAP, z.message)
    table = VMEM((z.groups,) + line, F32)
    counts = SMEM((z.groups,), jnp.int32)
    places_in = positions.transpose(1, 0, 2)
    to_left, center, to_right = call(
        run(pack_kernel, z),
        [((d,) + line, F32, VMEM)] * 3,
        [HBM] * 3,
        [
            SMEM(home_tile.shape, jnp.int32),
            SMEM(stiffness.shape, F32),
            VMEM(places_in.shape, F32),
            table,
            counts,
            pltpu.SemaphoreType.DMA((3,)),
        ],
    )(home_tile, stiffness, places_in)
    from_left = shift(to_right, "gx", 1)
    from_right = shift(to_left, "gx", -1)
    own = [jnp.stack([center[e], from_left[e], from_right[e]]) for e in range(d)]
    messages = {e: swap(own[e], "gy", e) for e in turns}
    messages = [own[0]] + [messages[e] for e in range(1, d)]
    near = neighbours.T
    link, degree, shape = call(
        run(matrix_kernel, z),
        [
            ((z.full, z.full), BF16, VMEM),
            ((1, z.full), F32, VMEM),
            ((3, z.full), F32, VMEM),
        ],
        [HBM, HBM, pl.ANY],
        [
            VMEM(near.shape, jnp.int32),
            VMEM(membrane_shape.shape, F32),
            VMEM((z.full, z.full), F32),
            pltpu.SemaphoreType.DMA((2,)),
        ],
        pl.CostEstimate(flops=2_000_000_000, bytes_accessed=4_000_000, transcendentals=0),
    )(near, membrane_shape, own[0])

    grid_type = ((3 * z.width_x, z.plane), F32, VMEM)
    post_type = ((19, z.width_x, z.plane), F32, VMEM)
    edge_types = [((8, z.plane), F32, VMEM)] * 2 + [((z.width_x, LANES), F32, VMEM)] * 2
    places_type = ((3, z.rows, z.full), F32, VMEM)
    lists = SMEM((LISTS,), jnp.int32)
    rows = VMEM(places_type[0], F32)
    flow = VMEM(grid_type[0], F32)
    edge = VMEM((z.width_x + 16, LANES), F32)

    grid, post, right, left, up, down, places, stiff = call(
        run(first_kernel, z),
        [grid_type, post_type] + edge_types + [places_type, ((z.slots, LANES), F32, VMEM)],
        [VMEM] * (d + 4),
        [VMEM((z.slots, LANES), F32), rows, lists] + buffer_types(z),
    )(*messages, shape, link, degree, populations)
    for _ in range(STEPS - 1):
        edges = trade_edges(z, right, left, up, down)
        grid, post, right, left, up, down, places = call(
            run(middle_kernel, z),
            [grid_type, post_type] + edge_types + [places_type],
            [VMEM] * 11,
            [VMEM(post_type[0], F32), flow, edge, edge, rows, lists] + buffer_types(z),
        )(post, *edges, grid, places, stiff, shape, link, degree)
    edges = trade_edges(z, right, left, up, down)
    moved, density, *messages = call(
        run(last_kernel, z),
        [post_type, grid_type] + [((3,) + line, F32, VMEM)] * d,
        [VMEM] * 8,
        [flow, edge, edge, rows, lists] + buffer_types(z),
    )(post, *edges, grid, places, stiff)
    back = {e: swap(messages[e], "gy", e) for e in turns}
    messages = [messages[0]] + [back[e] for e in range(1, d)]
    right_part = shift(jnp.stack([m[1] for m in messages]), "gx", -1)
    left_part = shift(jnp.stack([m[2] for m in messages]), "gx", 1)
    (displacement,) = call(
        run(unpack_kernel, z),
        [(places_in.shape, F32, VMEM)],
        [SMEM] + [VMEM] * (3 + d),
        [table, counts],
    )(home_tile, places_in, left_part, right_part, *messages)
    return moved, displacement.transpose(1, 0, 2), density.reshape(3, z.width_x, z.plane)


def solution(mesh):
    placed = (
        P(None, "gx", "gy"),
        P(("gx", "gy"), None, None),
        P(("gx", "gy")),
        P(),
        P(),
        P(("gx", "gy")),
    )
    return jax.shard_map(
        local,
        mesh=mesh,
        in_specs=placed,
        out_specs=(P(None, "gx", "gy"), P(("gx", "gy"), None, None), P(None, "gx", "gy")),
        check_vma=False,
    )
```
